256 devices in a mesh: head: 4 (over y_hi, core), seq: 64 (over x, y_lo, z).
Axes of the slice: x: 4, y: 4 (y_hi: 2, y_lo: 2; y = y_hi * 2 + y_lo), z: 8, core: 2. Of those that a mesh axis runs over, the one named last changes fastest.
Arguments:
- queries: bfloat16 [32768, 4096], P('seq', 'head'), may hold values from -6 to 6
- keys: bfloat16 [32768, 4096], P('seq', 'head'), may hold values from -6 to 6
- values: bfloat16 [32768, 4096], P('seq', 'head'), may hold values from -6 to 6
- rate: float32 [8, 32768], P('head', 'seq'), may hold values from 0.0001 to 0.001
- fast_gate: float32 [8, 512, 512], P('head', 'seq'), may hold values from -3 to 3
- fast_up: float32 [8, 512, 512], P('head', 'seq'), may hold values from -3 to 3
- fast_down: float32 [8, 512, 512], P('head', 'seq'), may hold values from -8 to 8
- out_gain: float32 [4096], P('head'), may hold values from 0.25 to 1.75
Outputs:
- mixed: bfloat16 [32768, 4096], P('seq', 'head')
- new_gate: float32 [8, 512, 512], P('head', 'seq')
- new_up: float32 [8, 512, 512], P('head', 'seq')
- new_down: float32 [8, 512, 512], P('head', 'seq')
The draws below stay inside these ranges and needn't reach their ends.
All inputs are finite; a program needn't handle non-finite values.
Results may differ from the reference program's by a relative error of at most 0.012.
Values may be sent and summed in bfloat16 or wider, within the bound.
No kernel may reach another device: no remote copies, remote signals or barrier semaphores. Data moves between devices by JAX's collectives and lax.ppermute only.
A program may use at most 128 MiB of HBM per device.

```python
import math
import jax
import jax.numpy as jnp
from jax import lax

HEADS = 8
HD = 512
FAST = 512
WINDOW = 512
GROUP = 32768


def query_key_pair(key):
    key_q, key_k = jax.random.split(jax.random.fold_in(key, 7), 2)
    width = HEADS * HD
    q_vals = 1.3 * jax.random.truncated_normal(key_q, -4.0, 4.0, (GROUP, width), jnp.float32)
    k_vals = 1.3 * jax.random.truncated_normal(key_k, -4.0, 4.0, (GROUP, width), jnp.float32)
    return (q_vals, k_vals)


def draw_queries(key, part):
    return query_key_pair(key)[0].astype(jnp.bfloat16)


def draw_keys(key, part):
    return query_key_pair(key)[1].astype(jnp.bfloat16)


def fast_matrix(key, salt, rows_n, cols_n, rising):
    key_base, key_cols = jax.random.split(jax.random.fold_in(key, salt))
    base = jax.random.truncated_normal(key_base, -4.0, 4.0, (HEADS, rows_n, cols_n), jnp.float32)
    row_scale = 10.0 ** (jnp.arange(rows_n, dtype=jnp.float32) / (rows_n - 1))
    col_scale = jnp.exp(jax.random.uniform(key_cols, (HEADS, 1, cols_n), jnp.float32, 0.0, math.log(10.0)))
    overall = jnp.sqrt(jnp.mean(row_scale * row_scale) * jnp.mean(col_scale * col_scale))
    if rising:
        head_scale = jnp.exp(jnp.arange(HEADS, dtype=jnp.float32) / max(HEADS - 1, 1) * math.log(3.0))
    else:
        head_scale = jnp.ones((HEADS,), jnp.float32)
    result = base * row_scale[None, :, None] * col_scale / overall / math.sqrt(rows_n)
    return (result * head_scale[:, None, None]).astype(jnp.float32)


def draw_fast_gate(key, part):
    return fast_matrix(key, 11, HD, FAST, False)


def draw_fast_up(key, part):
    return fast_matrix(key, 13, HD, FAST, False)


def draw_fast_down(key, part):
    return fast_matrix(key, 17, FAST, HD, True)


def block_scale(key, extent, cuts, least, high):
    loudness, own = 1.0, jax.random.fold_in(key, 6)
    for dim, blocks in cuts:
        heights = jnp.exp(jax.random.uniform(jax.random.fold_in(own, dim), (blocks,), jnp.float32, least / len(cuts), high / len(cuts)))
        loudness = loudness * jnp.repeat(heights, extent[dim] // blocks).reshape([-1 if axis == dim else 1 for axis in range(len(extent))])
    return loudness


def centred(key, dims, deviation, limit, cuts=(), kind=jnp.bfloat16):
    loudness = block_scale(key, dims, cuts, -0.22, 0.18) if cuts else 1.0
    values = jax.random.normal(key, dims, jnp.float32) * deviation * loudness
    return jnp.minimum(jnp.maximum(values, -limit), limit).astype(kind)


def setup_inputs(seed: int = 0) -> dict:
    key_list = jax.random.split(jax.random.key(seed), 9)
    return {
        "queries": draw_queries(jax.random.fold_in(key_list[8], 71), 0),
        "keys": draw_keys(jax.random.fold_in(key_list[8], 71), 0),
        "values": centred(key_list[2], (GROUP, HEADS * HD), 1.0, 6.0, ((0, 64), (1, 4))),
        "rate": jnp.clip(jnp.exp(math.log(0.001) - 2.3025852 * jax.random.uniform(key_list[3], (HEADS, GROUP), jnp.float32) ** block_scale(key_list[3], (HEADS, GROUP), ((0, 4), (1, 64)), -0.2, 0.2)), 0.0001, 0.001),
        "fast_gate": draw_fast_gate(jax.random.fold_in(key_list[8], 71), 0),
        "fast_up": draw_fast_up(jax.random.fold_in(key_list[8], 71), 0),
        "fast_down": draw_fast_down(jax.random.fold_in(key_list[8], 71), 0),
        "out_gain": jnp.clip(1.0 + 0.15 * jax.random.normal(key_list[7], (HEADS * HD,), jnp.float32), 0.25, 1.75),
    }


EPS = 1e-06

def rescale(old, upd):
    old_sq = lax.optimization_barrier(jnp.sum(old * old, axis=0))
    new_sq = lax.optimization_barrier(jnp.sum(upd * upd, axis=0))
    return upd * (jnp.sqrt(old_sq) / jnp.sqrt(new_sq + EPS))[None, :]

def head_update(inputs):
    qh, kh, vh, eta, w_one, w_three, w_two = inputs
    w1b = w_one.astype(jnp.bfloat16)
    w3b = w_three.astype(jnp.bfloat16)
    w2b = w_two.astype(jnp.bfloat16)
    pre_a = jnp.dot(kh, w1b, preferred_element_type=jnp.float32)
    pre_b = jnp.dot(kh, w3b, preferred_element_type=jnp.float32)
    sigma = jax.nn.sigmoid(pre_a)
    hidden = (pre_a * sigma * pre_b).astype(jnp.bfloat16)
    scaled = (eta[:, None] * vh.astype(jnp.float32)).astype(jnp.bfloat16)
    grad_two = jnp.dot(hidden.T, scaled, preferred_element_type=jnp.float32)
    back = jnp.dot(scaled, w2b.T, preferred_element_type=jnp.float32)
    d_gate = (back * pre_b * sigma * (1.0 + pre_a * (1.0 - sigma))).astype(jnp.bfloat16)
    d_up = (back * pre_a * sigma).astype(jnp.bfloat16)
    grad_one = jnp.dot(kh.T, d_gate, preferred_element_type=jnp.float32)
    grad_three = jnp.dot(kh.T, d_up, preferred_element_type=jnp.float32)
    new_one = rescale(w_one, w_one + grad_one)
    new_three = rescale(w_three, w_three + grad_three)
    new_two = rescale(w_two, w_two + grad_two)
    apply_a = jnp.dot(qh, new_one.astype(jnp.bfloat16), preferred_element_type=jnp.float32)
    apply_b = jnp.dot(qh, new_three.astype(jnp.bfloat16), preferred_element_type=jnp.float32)
    apply_h = (apply_a * jax.nn.sigmoid(apply_a) * apply_b).astype(jnp.bfloat16)
    result = jnp.dot(apply_h, new_two.astype(jnp.bfloat16), preferred_element_type=jnp.float32)
    return (result, new_one, new_three, new_two)

def reference(queries, keys, values, rate, fast_gate, fast_up, fast_down, out_gain):
    q_three = queries.reshape(GROUP, HEADS, HD)
    k_three = keys.reshape(GROUP, HEADS, HD)
    v_three = values.reshape(GROUP, HEADS, HD)
    lead = jnp.zeros((WINDOW, HEADS, HD), jnp.bfloat16)
    padded_k = jnp.concatenate([lead, k_three], axis=0)
    padded_v = jnp.concatenate([lead, v_three], axis=0)
    scale = 1.0 / math.sqrt(HD)
    rows_i = jnp.arange(WINDOW, dtype=jnp.int32)[:, None]
    cols_j = jnp.arange(2 * WINDOW, dtype=jnp.int32)[None, :]

    def attend(block):
        start = (block * WINDOW).astype(jnp.int32)
        q_blk = lax.dynamic_slice_in_dim(q_three, start, WINDOW, 0).astype(jnp.float32)
        k_blk = lax.dynamic_slice_in_dim(padded_k, start, 2 * WINDOW, 0).astype(jnp.float32)
        v_blk = lax.dynamic_slice_in_dim(padded_v, start, 2 * WINDOW, 0).astype(jnp.float32)
        scores = jnp.einsum('qhd,khd->hqk', q_blk, k_blk) * scale
        valid = (cols_j > rows_i) & (cols_j <= rows_i + WINDOW) & (start + cols_j >= WINDOW)
        scores = jnp.where(valid[None], scores, -jnp.inf)
        top = lax.optimization_barrier(jnp.max(scores, axis=-1, keepdims=True))
        expo = jnp.exp(scores - top)
        probs = (expo / lax.optimization_barrier(jnp.sum(expo, axis=-1, keepdims=True))).astype(jnp.bfloat16)
        return jnp.einsum('hqk,khd->qhd', probs.astype(jnp.float32), v_blk)
    attn = lax.map(attend, jnp.arange(GROUP // WINDOW, dtype=jnp.int32)).reshape(GROUP, HEADS, HD)
    result, new_gate, new_up, new_down = lax.map(head_update, (q_three.transpose(1, 0, 2), k_three.transpose(1, 0, 2), v_three.transpose(1, 0, 2), rate, fast_gate, fast_up, fast_down))
    branch = result.transpose(1, 0, 2)
    mean_sq = lax.optimization_barrier(jnp.mean(branch * branch, axis=(1, 2)))
    inv = lax.rsqrt(mean_sq + EPS)
    gain = out_gain.reshape(HEADS, HD)
    mixed = (attn + branch * inv[:, None, None] * gain[None]).astype(jnp.bfloat16)
    return (mixed.reshape(GROUP, HEADS * HD), new_gate, new_up, new_down)
```

```python
import functools
import math

import jax
import jax.numpy as jnp
from jax import lax
from jax.experimental import pallas as pl
from jax.experimental.pallas import tpu as pltpu
from jax.sharding import PartitionSpec as P

HEADS = 8
HD = 512
BLK = 512
EPS = 1e-06
NEG = -1e30
VMEM_LIMIT = 56 * 1024 * 1024
F32 = jnp.float32
BF16 = jnp.bfloat16

ZQ, XY = 4, 8


def move_xor(value, mask):
    n = lax.axis_size("seq")
    return lax.ppermute(value, "seq", [(i, i ^ mask) for i in range(n)])


def shift(value, step):
    n = lax.axis_size("seq")
    return lax.ppermute(value, "seq", [(i, (i + step) % n) for i in range(n)])


def dot(a, b):
    return lax.dot_general(a, b, (((1,), (0,)), ((), ())), preferred_element_type=F32)


def dot_rows(a, b):
    return lax.dot_general(a, b, (((0,), (0,)), ((), ())), preferred_element_type=F32)


def dot_cols(a, b):
    return lax.dot_general(a, b, (((1,), (1,)), ((), ())), preferred_element_type=F32)


def whole(shape):
    rank = len(shape)
    return pl.BlockSpec(shape, lambda i, s: (0,) * rank)


def head_block(pick):
    return pl.BlockSpec((BLK, HD), lambda i, s: (0, s[pick]))


def call(kernel, scalars, ins, in_specs, outs, scratch=(), flops=0):
    multi = isinstance(outs, list)
    out_list = outs if multi else [outs]
    nbytes = sum(a.size * a.dtype.itemsize for a in ins)
    specs = [whole(o.shape) for o in out_list]
    return pl.pallas_call(
        kernel,
        out_shape=outs,
        grid_spec=pltpu.PrefetchScalarGridSpec(
            num_scalar_prefetch=1,
            grid=(1,),
            in_specs=in_specs,
            out_specs=specs if multi else specs[0],
            scratch_shapes=list(scratch),
        ),
        compiler_params=pltpu.CompilerParams(vmem_limit_bytes=VMEM_LIMIT),
        cost_estimate=pl.CostEstimate(flops=flops, transcendentals=0, bytes_accessed=nbytes),
    )(scalars, *ins)


def row_start(s_ref, index):
    return pl.multiple_of(s_ref[index], 16)


def fill_rows(s_ref, blocks, rows_ref):
    for j, block in enumerate(blocks):
        for k in range(ZQ):
            at = pl.multiple_of(row_start(s_ref, 4 + j) + row_start(s_ref, 12 + k), 16)
            for m in range(3):
                rows_ref[m, pl.ds(at, 16), :] = block[k, m]


def columns_sq(rows_ref, m):
    w = rows_ref[m].astype(F32)
    return jnp.sum(w * w, axis=0, keepdims=True)


def as_column(row):
    return jnp.broadcast_to(row, (128, row.shape[1])).T


def gradient_kernel(s_ref, halo, k_own, v_own, rate_prev, rate_own, *rest):
    blocks, rest = rest[:XY], rest[XY:]
    own_out, outs, old_sq = rest[0], rest[1:XY], rest[XY]
    w_rows, k_all, gv, hid, d_gate, d_up, grads = rest[XY + 1:]
    fill_rows(s_ref, blocks, w_rows)
    for m in range(3):
        old_sq[m:m + 1, :] = columns_sq(w_rows, m)
    for part in range(2):
        rows = slice(part * BLK, (part + 1) * BLK)
        k = halo[0] if part == 0 else k_own[...]
        v = (halo[1] if part == 0 else v_own[...]).astype(F32)
        eta = as_column((rate_prev if part == 0 else rate_own)[0:1, :])
        scaled = jnp.concatenate(
            [eta * v[:, c * 128:(c + 1) * 128] for c in range(HD // 128)], axis=1
        ).astype(BF16)
        k_all[rows, :] = k
        gv[rows, :] = scaled
        pre_a = dot(k, w_rows[0])
        pre_b = dot(k, w_rows[1])
        back = dot_cols(scaled, w_rows[2])
        sigma = jax.nn.sigmoid(pre_a)
        gated = pre_a * sigma
        hid[rows, :] = (gated * pre_b).astype(BF16)
        d_gate[rows, :] = (back * pre_b * sigma * (1.0 + pre_a * (1.0 - sigma))).astype(BF16)
        d_up[rows, :] = (back * gated).astype(BF16)
    grads[0] = dot_rows(k_all[...], d_gate[...])
    grads[1] = dot_rows(k_all[...], d_up[...])
    grads[2] = dot_rows(hid[...], gv[...])
    for m in range(3):
        own_out[m] = grads[m, pl.ds(row_start(s_ref, 4), 64), :]
        for j, out in enumerate(outs):
            out[m] = grads[m, pl.ds(row_start(s_ref, 5 + j), 64), :].astype(BF16)


def block_sum_kernel(s_ref, own, *rest):
    parts, outs, total = rest[:XY - 1], rest[XY - 1:XY - 1 + ZQ], rest[-1]
    acc = own[...]
    for part in parts:
        acc = acc + part[...].astype(F32)
    total[...] = acc
    for m in range(3):
        for k, out in enumerate(outs):
            out[m] = total[m, pl.ds(row_start(s_ref, 12 + k), 16), :].astype(out.dtype)


def update_kernel(s_ref, own, one, two, three, w_own, upd, upd_b):
    total = own[...] + one[...].astype(F32) + two[...].astype(F32) + three[...].astype(F32)
    total = total + w_own[...]
    upd[...] = total
    upd_b[...] = total.astype(BF16)


def apply_kernel(s_ref, q_prev, q_own, old_sq, upd, *rest):
    blocks, rest = rest[:XY], rest[XY:]
    f_prev, f_own, sq, new, u_rows = rest
    fill_rows(s_ref, blocks, u_rows)
    ratio = [
        jnp.sqrt(old_sq[m:m + 1, :]) / jnp.sqrt(columns_sq(u_rows, m) + EPS) for m in range(3)
    ]
    for m in range(3):
        new[m] = upd[m] * ratio[m]
    for part, (q, out) in enumerate(((q_prev, f_prev), (q_own, f_own))):
        pre_a = dot(q[...], u_rows[0]) * ratio[0]
        pre_b = dot(q[...], u_rows[1]) * ratio[1]
        hid = (pre_a * jax.nn.sigmoid(pre_a) * pre_b).astype(BF16)
        branch = dot(hid, u_rows[2]) * ratio[2]
        out[...] = branch.astype(BF16)
        squares = branch * branch
        lanes = sum(squares[:, c * 128:(c + 1) * 128] for c in range(HD // 128))
        sq[part:part + 1, :] = jnp.sum(lanes.T, axis=0, keepdims=True)


def attention_kernel(s_ref, q_ref, k_ref, v_ref, halo, out):
    scale = 1.0 / math.sqrt(HD)
    first = s_ref[2] == 0
    half = BLK // 2
    for part in range(2):
        base = part * half
        q = q_ref[base:base + half, :]
        own_len = base + half
        prev_len = BLK - base
        s_prev = dot_cols(q, halo[0, base:, :]) * scale
        s_own = dot_cols(q, k_ref[:own_len, :]) * scale
        row_p = lax.broadcasted_iota(jnp.int32, (half, prev_len), 0)
        col_p = lax.broadcasted_iota(jnp.int32, (half, prev_len), 1)
        keep_p = jnp.logical_and(col_p > row_p, jnp.logical_not(first))
        row_o = lax.broadcasted_iota(jnp.int32, (half, own_len), 0) + base
        col_o = lax.broadcasted_iota(jnp.int32, (half, own_len), 1)
        s_prev = jnp.where(keep_p, s_prev, NEG)
        s_own = jnp.where(col_o <= row_o, s_own, NEG)
        top = jnp.maximum(
            jnp.max(s_prev, axis=1, keepdims=True), jnp.max(s_own, axis=1, keepdims=True)
        )
        e_prev = jnp.exp(s_prev - top)
        e_own = jnp.exp(s_own - top)
        inv = 1.0 / (
            jnp.sum(e_prev, axis=1, keepdims=True) + jnp.sum(e_own, axis=1, keepdims=True)
        )
        p_prev = (e_prev * inv).astype(BF16)
        p_own = (e_own * inv).astype(BF16)
        out[base:base + half, :] = dot(p_prev, halo[1, base:, :]) + dot(p_own, v_ref[:own_len, :])


def mix_kernel(s_ref, f_own, f_back, attn_own, attn_other, sums, gain, out):
    inv = as_column(lax.rsqrt(sums[0:1, :] / (HEADS * HD) + EPS))
    for own_head in range(2):

        @pl.when(s_ref[0] == own_head)
        def _():
            for head in range(2):
                f, attn = (f_own, attn_own) if head == own_head else (f_back, attn_other)
                for c in range(HD // 128):
                    cols = slice(c * 128, (c + 1) * 128)
                    to = slice(head * HD + c * 128, head * HD + (c + 1) * 128)
                    branch = f[:, cols].astype(F32) * inv * gain[0:1, to]
                    out[:, to] = (attn[:, cols] + branch).astype(BF16)


def shape(dims, dtype):
    return jax.ShapeDtypeStruct(dims, dtype)


def local(queries, keys, values, rate, fast_gate, fast_up, fast_down, out_gain):
    seq_pos = lax.axis_index("seq").astype(jnp.int32)
    own = seq_pos & 1
    other = 1 - own
    zq = (seq_pos >> 1) & (ZQ - 1)
    xy = seq_pos >> 3
    scalars = jnp.stack(
        [own, other, seq_pos, seq_pos * 0]
        + [64 * (xy ^ j) for j in range(XY)]
        + [16 * (zq ^ k) for k in range(ZQ)]
    ).astype(jnp.int32)
    even = own == 0

    def head_of(array, want_own):
        flag = even if want_own else jnp.logical_not(even)
        return jnp.where(flag, array[:, :HD], array[:, HD:])

    fast = jnp.stack([fast_gate, fast_up, fast_down])
    mine = jnp.where(even, fast[:, 0], fast[:, 1])
    theirs = jnp.where(even, fast[:, 1], fast[:, 0])
    got = move_xor(theirs, 1)
    w_pair = jnp.where(
        even, jnp.concatenate([mine, got], axis=1), jnp.concatenate([got, mine], axis=1)
    )

    halo_send = jnp.stack([head_of(keys, False), head_of(values, False)])
    rate_send = jnp.where(even, rate[1:2], rate[0:1])
    rate_mine = jnp.where(even, rate[0:1], rate[1:2])

    def gather_blocks(chunk):
        block = jnp.stack([chunk] + [move_xor(chunk, k << 1) for k in range(1, ZQ)])
        return [block] + [move_xor(block, j << 3) for j in range(1, XY)]

    w_blocks = gather_blocks(w_pair.astype(BF16))
    halo = shift(halo_send, 1)
    rate_prev = shift(rate_send, 1)

    block_specs = [whole((ZQ, 3, 16, HD))] * XY
    grad_out = call(
        gradient_kernel,
        scalars,
        [halo, keys, values, rate_prev, rate_mine] + w_blocks,
        [whole((2, BLK, HD)), head_block(0), head_block(0), whole((1, BLK)), whole((1, BLK))]
        + block_specs,
        [shape((3, 64, HD), F32)] + [shape((3, 64, HD), BF16)] * (XY - 1) + [shape((3, HD), F32)],
        [pltpu.VMEM((3, HD, HD), BF16)]
        + [pltpu.VMEM((2 * BLK, HD), BF16)] * 5
        + [pltpu.VMEM((3, HD, HD), F32)],
        flops=12 * 2 * BLK * HD * HD,
    )
    old_sq = grad_out[XY]
    arrived = [move_xor(grad_out[j], j << 3) for j in range(1, XY)]
    chunks = call(
        block_sum_kernel,
        scalars,
        [grad_out[0]] + arrived,
        [whole((3, 64, HD))] * XY,
        [shape((3, 16, HD), F32)] + [shape((3, 16, HD), BF16)] * (ZQ - 1),
        [pltpu.VMEM((3, 64, HD), F32)],
    )
    arrived = [move_xor(chunks[k], k << 1) for k in range(1, ZQ)]
    upd, upd_b = call(
        update_kernel,
        scalars,
        [chunks[0]] + arrived + [w_pair],
        [whole((3, 16, HD))] * 5,
        [shape((3, 16, HD), F32), shape((3, 16, HD), BF16)],
    )
    u_blocks = gather_blocks(upd_b)

    halo_other = shift(jnp.stack([head_of(keys, True), head_of(values, True)]), 1)
    q_prev = shift(head_of(queries, False), 1)

    def attend(pick, prev):
        return call(
            attention_kernel,
            scalars,
            [queries, keys, values, prev],
            [head_block(pick)] * 3 + [whole((2, BLK, HD))],
            shape((BLK, HD), F32),
            flops=4 * BLK * 768 * HD,
        )

    attn_own = attend(0, halo)
    attn_other = attend(1, halo_other)

    f_prev, f_own, sq, new = call(
        apply_kernel,
        scalars,
        [q_prev, queries, old_sq, upd] + u_blocks,
        [whole((BLK, HD)), head_block(0), whole((3, HD)), whole((3, 16, HD))] + block_specs,
        [
            shape((BLK, HD), BF16),
            shape((BLK, HD), BF16),
            shape((2, BLK), F32),
            shape((3, 16, HD), F32),
        ],
        [pltpu.VMEM((3, HD, HD), BF16)],
        flops=6 * 2 * BLK * HD * HD,
    )
    f_back = shift(f_prev, -1)
    heads = lax.axis_size("head")
    totals = sq
    for k in range(1, heads):
        totals = totals + lax.ppermute(sq, "head", [(i, i ^ k) for i in range(heads)])
    sums = totals[1:2] + shift(totals[0:1], -1)
    new_mine = jnp.where(even, new[:, :8], new[:, 8:])
    new_theirs = move_xor(jnp.where(even, new[:, 8:], new[:, :8]), 1)
    new_all = jnp.where(
        even,
        jnp.stack([new_mine, new_theirs], axis=1),
        jnp.stack([new_theirs, new_mine], axis=1),
    )
    mixed = call(
        mix_kernel,
        scalars,
        [f_own, f_back, attn_own, attn_other, sums, out_gain.reshape(1, 2 * HD)],
        [whole((BLK, HD))] * 4 + [whole((1, BLK)), whole((1, 2 * HD))],
        shape((BLK, 2 * HD), BF16),
    )
    return mixed, new_all[0], new_all[1], new_all[2]


def solution(mesh):
    tokens = P("seq", "head")
    fast = P("head", "seq", None)
    return jax.shard_map(
        local,
        mesh=mesh,
        in_specs=(tokens, tokens, tokens, P("head", "seq"), fast, fast, fast, P("head")),
        out_specs=(tokens, fast, fast, fast),
        check_vma=False,
    )
```

```python
import functools
import math

import jax
import jax.numpy as jnp
from jax import lax
from jax.experimental import pallas as pl
from jax.experimental.pallas import tpu as pltpu
from jax.sharding import PartitionSpec as P

HEADS = 8
HD = 512
BLK = 512
EPS = 1e-06
NEG = -1e30
VMEM_LIMIT = 56 * 1024 * 1024
F32 = jnp.float32
BF16 = jnp.bfloat16

ZQ, XY, RING = 4, 8, 8


def move_xor(value, mask):
    n = lax.axis_size("seq")
    return lax.ppermute(value, "seq", [(i, i ^ mask) for i in range(n)])


def ring(value, step):
    n = lax.axis_size("seq")
    pairs = [(i, i - i % RING + (i + step) % RING) for i in range(n)]
    return lax.ppermute(value, "seq", pairs)


def to_next_plane(value):
    n = lax.axis_size("seq")
    return lax.ppermute(value, "seq", [(i, i + RING) for i in range(RING - 1, n - RING, RING)])


def close_ring(value):
    n = lax.axis_size("seq")
    return lax.ppermute(value, "seq", [(i, i - RING + 1) for i in range(RING - 1, n, RING)])


def after(value, other):
    return lax.optimization_barrier((value, other))[0]


def dot(a, b):
    return lax.dot_general(a, b, (((1,), (0,)), ((), ())), preferred_element_type=F32)


def dot_rows(a, b):
    return lax.dot_general(a, b, (((0,), (0,)), ((), ())), preferred_element_type=F32)


def dot_cols(a, b):
    return lax.dot_general(a, b, (((1,), (1,)), ((), ())), preferred_element_type=F32)


def whole(shape):
    rank = len(shape)
    return pl.BlockSpec(shape, lambda i, s: (0,) * rank)


def head_block(pick):
    return pl.BlockSpec((BLK, HD), lambda i, s: (0, s[pick]))


def call(kernel, scalars, ins, in_specs, outs, scratch=(), flops=0):
    multi = isinstance(outs, list)
    out_list = outs if multi else [outs]
    nbytes = sum(a.size * a.dtype.itemsize for a in ins)
    specs = [whole(o.shape) for o in out_list]
    return pl.pallas_call(
        kernel,
        out_shape=outs,
        grid_spec=pltpu.PrefetchScalarGridSpec(
            num_scalar_prefetch=1,
            grid=(1,),
            in_specs=in_specs,
            out_specs=specs if multi else specs[0],
            scratch_shapes=list(scratch),
        ),
        compiler_params=pltpu.CompilerParams(vmem_limit_bytes=VMEM_LIMIT),
        cost_estimate=pl.CostEstimate(flops=flops, transcendentals=0, bytes_accessed=nbytes),
    )(scalars, *ins)


def row_start(s_ref, index):
    return pl.multiple_of(s_ref[index], 16)


def fill_rows(s_ref, blocks, rows_ref):
    for j, block in enumerate(blocks):
        for t in range(2):
            for k in range(ZQ):
                at = row_start(s_ref, 4 + 2 * j + t) + row_start(s_ref, 12 + k)
                at = pl.multiple_of(at, 16)
                for m in range(3):
                    rows_ref[m, pl.ds(at, 16), :] = block[t, k, m]


def columns_sq(rows_ref, m):
    w = rows_ref[m].astype(F32)
    return jnp.sum(w * w, axis=0, keepdims=True)


def as_column(row):
    return jnp.broadcast_to(row, (128, row.shape[1])).T


def gradient_kernel(s_ref, halo, k_own, v_own, rate_prev, rate_own, *rest):
    blocks, rest = rest[:XY // 2], rest[XY // 2:]
    own_out, outs, old_sq = rest[0], rest[1:XY], rest[XY]
    w_rows, k_all, gv, hid, d_gate, d_up, grads = rest[XY + 1:]
    fill_rows(s_ref, blocks, w_rows)
    for m in range(3):
        old_sq[m:m + 1, :] = columns_sq(w_rows, m)
    for part in range(2):
        rows = slice(part * BLK, (part + 1) * BLK)
        k = halo[0] if part == 0 else k_own[...]
        v = (halo[1] if part == 0 else v_own[...]).astype(F32)
        eta = as_column((rate_prev if part == 0 else rate_own)[0:1, :])
        scaled = jnp.concatenate(
            [eta * v[:, c * 128:(c + 1) * 128] for c in range(HD // 128)], axis=1
        ).astype(BF16)
        k_all[rows, :] = k
        gv[rows, :] = scaled
        pre_a = dot(k, w_rows[0])
        pre_b = dot(k, w_rows[1])
        back = dot_cols(scaled, w_rows[2])
        sigma = jax.nn.sigmoid(pre_a)
        gated = pre_a * sigma
        hid[rows, :] = (gated * pre_b).astype(BF16)
        d_gate[rows, :] = (back * pre_b * sigma * (1.0 + pre_a * (1.0 - sigma))).astype(BF16)
        d_up[rows, :] = (back * gated).astype(BF16)
    grads[0] = dot_rows(k_all[...], d_gate[...])
    grads[1] = dot_rows(k_all[...], d_up[...])
    grads[2] = dot_rows(hid[...], gv[...])
    for m in range(3):
        own_out[m] = grads[m, pl.ds(row_start(s_ref, 4), 64), :]
        for j, out in enumerate(outs):
            out[m] = grads[m, pl.ds(row_start(s_ref, 5 + j), 64), :].astype(BF16)


def block_sum_kernel(s_ref, own, *rest):
    parts, outs, total = rest[:XY - 1], rest[XY - 1:XY - 1 + ZQ], rest[-1]
    acc = own[...]
    for part in parts:
        acc = acc + part[...].astype(F32)
    total[...] = acc
    for m in range(3):
        for k, out in enumerate(outs):
            out[m] = total[m, pl.ds(row_start(s_ref, 12 + k), 16), :].astype(out.dtype)


def update_kernel(s_ref, own, one, two, three, w_own, upd, upd_b):
    total = own[...] + one[...].astype(F32) + two[...].astype(F32) + three[...].astype(F32)
    total = total + w_own[...]
    upd[...] = total
    upd_b[...] = total.astype(BF16)


def branch_of(q, u_rows, ratio):
    pre_a = dot(q, u_rows[0]) * ratio[0]
    pre_b = dot(q, u_rows[1]) * ratio[1]
    hid = (pre_a * jax.nn.sigmoid(pre_a) * pre_b).astype(BF16)
    branch = dot(hid, u_rows[2]) * ratio[2]
    squares = branch * branch
    lanes = sum(squares[:, c * 128:(c + 1) * 128] for c in range(HD // 128))
    return branch.astype(BF16), jnp.sum(lanes.T, axis=0, keepdims=True)


def apply_kernel(s_ref, q_prev, q_own, old_sq, upd, *rest):
    blocks, (f_prev, f_own, sq, new, u_rows) = rest[:XY // 2], rest[XY // 2:]
    fill_rows(s_ref, blocks, u_rows)
    ratio = [
        jnp.sqrt(old_sq[m:m + 1, :]) / jnp.sqrt(columns_sq(u_rows, m) + EPS) for m in range(3)
    ]
    for m in range(3):
        new[m] = upd[m] * ratio[m]
    f_prev[...], sq[0:1, :] = branch_of(q_prev[...], u_rows, ratio)
    f_own[...], sq[1:2, :] = branch_of(q_own[...], u_rows, ratio)


def attention_kernel(s_ref, q_ref, k_ref, v_ref, halo, *rest):
    scale = 1.0 / math.sqrt(HD)
    first = s_ref[2] == 0
    crossing = s_ref[3] == 0
    close, out = rest[:-1], rest[-1]
    half = BLK // 2
    for part in range(2):
        base = part * half
        q = q_ref[base:base + half, :]
        own_len = base + half
        prev_len = BLK - base
        k_prev, v_prev = halo[0, base:, :], halo[1, base:, :]
        if close:
            k_prev = jnp.where(crossing, close[0][0, base:, :], k_prev)
            v_prev = jnp.where(crossing, close[0][1, base:, :], v_prev)
        s_prev = dot_cols(q, k_prev) * scale
        s_own = dot_cols(q, k_ref[:own_len, :]) * scale
        row_p = lax.broadcasted_iota(jnp.int32, (half, prev_len), 0)
        col_p = lax.broadcasted_iota(jnp.int32, (half, prev_len), 1)
        keep_p = jnp.logical_and(col_p > row_p, jnp.logical_not(first))
        row_o = lax.broadcasted_iota(jnp.int32, (half, own_len), 0) + base
        col_o = lax.broadcasted_iota(jnp.int32, (half, own_len), 1)
        s_prev = jnp.where(keep_p, s_prev, NEG)
        s_own = jnp.where(col_o <= row_o, s_own, NEG)
        top = jnp.maximum(
            jnp.max(s_prev, axis=1, keepdims=True), jnp.max(s_own, axis=1, keepdims=True)
        )
        e_prev = jnp.exp(s_prev - top)
        e_own = jnp.exp(s_own - top)
        inv = 1.0 / (
            jnp.sum(e_prev, axis=1, keepdims=True) + jnp.sum(e_own, axis=1, keepdims=True)
        )
        p_prev = (e_prev * inv).astype(BF16)
        p_own = (e_own * inv).astype(BF16)
        out[base:base + half, :] = dot(p_prev, v_prev) + dot(p_own, v_ref[:own_len, :])


def mix_kernel(s_ref, f_own, f_back, attn_own, attn_other, sums, gain, out):
    inv = as_column(lax.rsqrt(sums[0:1, :] / (HEADS * HD) + EPS))
    for own_head in range(2):

        @pl.when(s_ref[0] == own_head)
        def _():
            for head in range(2):
                f, attn = (f_own, attn_own) if head == own_head else (f_back, attn_other)
                for c in range(HD // 128):
                    cols = slice(c * 128, (c + 1) * 128)
                    to = slice(head * HD + c * 128, head * HD + (c + 1) * 128)
                    branch = f[:, cols].astype(F32) * inv * gain[0:1, to]
                    out[:, to] = (attn[:, cols] + branch).astype(BF16)


def shape(dims, dtype):
    return jax.ShapeDtypeStruct(dims, dtype)


def local(queries, keys, values, rate, fast_gate, fast_up, fast_down, out_gain):
    seq_pos = lax.axis_index("seq").astype(jnp.int32)
    own = seq_pos & 1
    other = 1 - own
    zq = (seq_pos >> 1) & (ZQ - 1)
    xy = seq_pos >> 3
    scalars = jnp.stack(
        [own, other, seq_pos, seq_pos & (RING - 1)]
        + [64 * (xy ^ j) for j in range(XY)]
        + [16 * (zq ^ k) for k in range(ZQ)]
    ).astype(jnp.int32)
    even = own == 0

    def head_of(array, want_own):
        flag = even if want_own else jnp.logical_not(even)
        return jnp.where(flag, array[:, :HD], array[:, HD:])

    fast = jnp.stack([fast_gate, fast_up, fast_down])
    mine = jnp.where(even, fast[:, 0], fast[:, 1])
    theirs = jnp.where(even, fast[:, 1], fast[:, 0])
    got = move_xor(theirs, 1)
    w_pair = jnp.where(
        even, jnp.concatenate([mine, got], axis=1), jnp.concatenate([got, mine], axis=1)
    )

    rate_send = jnp.where(even, rate[1:2], rate[0:1])
    rate_mine = jnp.where(even, rate[0:1], rate[1:2])

    def gather_zq(chunk):
        return jnp.stack([chunk] + [move_xor(chunk, k << 1) for k in range(1, ZQ)])

    def gather_xy(block):
        pair = jnp.stack([block, move_xor(block, 1 << 3)])
        return [pair] + [move_xor(pair, j << 4) for j in range(1, XY // 2)]

    send_other = jnp.stack([head_of(keys, False), head_of(values, False)])
    send_own = jnp.stack([head_of(keys, True), head_of(values, True)])
    plane_k = to_next_plane(keys[:, HD:])
    rate_prev = ring(rate_send, 1)
    w_block = after(gather_zq(after(w_pair.astype(BF16), rate_prev)), plane_k)
    w_blocks = gather_xy(w_block)
    halo = ring(after(send_other, w_block), 1)
    last = (seq_pos & (RING - 1)) == RING - 1
    plane_v = to_next_plane(after(values[:, HD:], w_blocks[-1]))
    q_prev = ring(after(head_of(queries, False), halo), 1)

    def attend(pick, prev):
        return call(
            attention_kernel,
            scalars,
            [queries, keys, values] + prev,
            [head_block(pick)] * 3 + [whole((2, BLK, HD))] * len(prev),
            shape((BLK, HD), F32),
            flops=4 * BLK * 768 * HD,
        )

    block_specs = [whole((2, ZQ, 3, 16, HD))] * (XY // 2)
    grad_out = call(
        gradient_kernel,
        scalars,
        [halo, keys, values, rate_prev, rate_mine] + w_blocks,
        [whole((2, BLK, HD)), head_block(0), head_block(0), whole((1, BLK)), whole((1, BLK))]
        + block_specs,
        [shape((3, 64, HD), F32)] + [shape((3, 64, HD), BF16)] * (XY - 1) + [shape((3, HD), F32)],
        [pltpu.VMEM((3, HD, HD), BF16)]
        + [pltpu.VMEM((2 * BLK, HD), BF16)] * 5
        + [pltpu.VMEM((3, HD, HD), F32)],
        flops=12 * 2 * BLK * HD * HD,
    )
    old_sq = grad_out[XY]
    arrived = [move_xor(grad_out[j], j << 3) for j in range(1, XY)]
    plane_own = jnp.stack([plane_k, after(plane_v, old_sq)])
    halo_other = ring(jnp.where(last, plane_own, after(send_own, q_prev)), 1)
    chunks = call(
        block_sum_kernel,
        scalars,
        [grad_out[0]] + arrived,
        [whole((3, 64, HD))] * XY,
        [shape((3, 16, HD), F32)] + [shape((3, 16, HD), BF16)] * (ZQ - 1),
        [pltpu.VMEM((3, 64, HD), F32)],
    )
    arrived = [move_xor(chunks[k], k << 1) for k in range(1, ZQ)]
    upd, upd_b = call(
        update_kernel,
        scalars,
        [after(chunks[0], halo_other)] + arrived + [w_pair],
        [whole((3, 16, HD))] * 5,
        [shape((3, 16, HD), F32), shape((3, 16, HD), BF16)],
    )
    plane_other = to_next_plane(after(send_other, chunks[0]))
    u_block = after(gather_zq(upd_b), plane_other)
    u_blocks = gather_xy(u_block)
    closing = close_ring(after(plane_other, u_block))
    attn_other = attend(1, [halo_other])
    attn_own = attend(0, [halo, closing])
    f_prev, f_own, sq, new = call(
        apply_kernel,
        scalars,
        [after(after(q_prev, attn_other), attn_own), queries, old_sq, upd] + u_blocks,
        [whole((BLK, HD)), head_block(0), whole((3, HD)), whole((3, 16, HD))] + block_specs,
        [
            shape((BLK, HD), BF16),
            shape((BLK, HD), BF16),
            shape((2, BLK), F32),
            shape((3, 16, HD), F32),
        ],
        [pltpu.VMEM((3, HD, HD), BF16)],
        flops=6 * 2 * BLK * HD * HD,
    )
    f_back = ring(f_prev, -1)
    heads = lax.axis_size("head")
    totals = sq
    for k in range(1, heads):
        totals = totals + lax.ppermute(sq, "head", [(i, i ^ k) for i in range(heads)])
    sums = totals[1:2] + ring(totals[0:1], -1)
    new_mine = jnp.where(even, new[:, :8], new[:, 8:])
    new_theirs = after(move_xor(jnp.where(even, new[:, 8:], new[:, :8]), 1), f_back)
    new_all = jnp.where(
        even,
        jnp.stack([new_mine, new_theirs], axis=1),
        jnp.stack([new_theirs, new_mine], axis=1),
    )
    mixed = call(
        mix_kernel,
        scalars,
        [f_own, f_back, attn_own, attn_other, sums, out_gain.reshape(1, 2 * HD)],
        [whole((BLK, HD))] * 4 + [whole((1, BLK)), whole((1, 2 * HD))],
        shape((BLK, 2 * HD), BF16),
    )
    return mixed, new_all[0], new_all[1], new_all[2]


def solution(mesh):
    tokens = P("seq", "head")
    fast = P("head", "seq", None)
    return jax.shard_map(
        local,
        mesh=mesh,
        in_specs=(tokens, tokens, tokens, P("head", "seq"), fast, fast, fast, P("head")),
        out_specs=(tokens, fast, fast, fast),
        check_vma=False,
    )
```

```python
import functools
import math

import jax
import jax.numpy as jnp
from jax import lax
from jax.experimental import pallas as pl
from jax.experimental.pallas import tpu as pltpu
from jax.sharding import PartitionSpec as P

HEADS = 8
HD = 512
BLK = 512
TILE = 512
EPS = 1e-06
NEG = -1e30
VMEM_LIMIT = 56 * 1024 * 1024
F32 = jnp.float32
BF16 = jnp.bfloat16

ZQ, XY, RING = 4, 8, 8


def move_xor(value, mask):
    n = lax.axis_size("seq")
    return lax.ppermute(value, "seq", [(i, i ^ mask) for i in range(n)])


def ring(value, step):
    n = lax.axis_size("seq")
    pairs = [(i, i - i % RING + (i + step) % RING) for i in range(n)]
    return lax.ppermute(value, "seq", pairs)


def to_next_plane(value):
    n = lax.axis_size("seq")
    return lax.ppermute(value, "seq", [(i, i + RING) for i in range(RING - 1, n - RING, RING)])


def close_ring(value):
    n = lax.axis_size("seq")
    return lax.ppermute(value, "seq", [(i, i - RING + 1) for i in range(RING - 1, n, RING)])


def after(value, other):
    return lax.optimization_barrier((value, other))[0]


def dot(a, b):
    return lax.dot_general(a, b, (((1,), (0,)), ((), ())), preferred_element_type=F32)


def dot_rows(a, b):
    return lax.dot_general(a, b, (((0,), (0,)), ((), ())), preferred_element_type=F32)


def dot_cols(a, b):
    return lax.dot_general(a, b, (((1,), (1,)), ((), ())), preferred_element_type=F32)


def whole(shape):
    rank = len(shape)
    return pl.BlockSpec(shape, lambda i, s: (0,) * rank)


def head_block(pick):
    return pl.BlockSpec((BLK, HD), lambda i, s: (0, s[pick]))


def call(kernel, scalars, ins, in_specs, outs, scratch=(), flops=0):
    multi = isinstance(outs, list)
    out_list = outs if multi else [outs]
    nbytes = sum(a.size * a.dtype.itemsize for a in ins)
    specs = [whole(o.shape) for o in out_list]
    return pl.pallas_call(
        kernel,
        out_shape=outs,
        grid_spec=pltpu.PrefetchScalarGridSpec(
            num_scalar_prefetch=1,
            grid=(1,),
            in_specs=in_specs,
            out_specs=specs if multi else specs[0],
            scratch_shapes=list(scratch),
        ),
        compiler_params=pltpu.CompilerParams(vmem_limit_bytes=VMEM_LIMIT),
        cost_estimate=pl.CostEstimate(flops=flops, transcendentals=0, bytes_accessed=nbytes),
    )(scalars, *ins)


def row_start(s_ref, index):
    return pl.multiple_of(s_ref[index], 16)


def fill_rows(s_ref, blocks, rows_ref):
    for j, block in enumerate(blocks):
        for t in range(2):
            for k in range(ZQ):
                at = row_start(s_ref, 4 + 2 * j + t) + row_start(s_ref, 12 + k)
                at = pl.multiple_of(at, 16)
                for m in range(3):
                    rows_ref[m, pl.ds(at, 16), :] = block[t, k, m]


def columns_sq(rows_ref, m):
    w = rows_ref[m].astype(F32)
    return jnp.sum(w * w, axis=0, keepdims=True)


def as_column(row):
    return jnp.broadcast_to(row, (128, row.shape[1])).T


def gradient_kernel(s_ref, halo, k_own, v_own, rate_prev, rate_own, *rest):
    blocks, rest = rest[:XY // 2], rest[XY // 2:]
    own_out, outs, old_sq = rest[0], rest[1:XY], rest[XY]
    w_rows, k_all, gv, hid, d_both, grads = rest[XY + 1:]
    fill_rows(s_ref, blocks, w_rows)
    for m in range(3):
        old_sq[m:m + 1, :] = columns_sq(w_rows, m)
    for part in range(2):
        eta_all = as_column((rate_prev if part == 0 else rate_own)[0:1, :])
        for at in range(0, BLK, TILE):
            rows = slice(part * BLK + at, part * BLK + at + TILE)
            here = slice(at, at + TILE)
            k = halo[0, here, :] if part == 0 else k_own[here, :]
            v = (halo[1, here, :] if part == 0 else v_own[here, :]).astype(F32)
            eta = eta_all[here, :]
            scaled = jnp.concatenate(
                [eta * v[:, c * 128:(c + 1) * 128] for c in range(HD // 128)], axis=1
            ).astype(BF16)
            k_all[rows, :] = k
            gv[rows, :] = scaled
            pre_a = dot(k, w_rows[0])
            pre_b = dot(k, w_rows[1])
            back = dot_cols(scaled, w_rows[2])
            sigma = jax.nn.sigmoid(pre_a)
            gated = pre_a * sigma
            hid[rows, :] = (gated * pre_b).astype(BF16)
            gate = back * pre_b * sigma * (1.0 + pre_a * (1.0 - sigma))
            d_both[rows, :HD] = gate.astype(BF16)
            d_both[rows, HD:] = (back * gated).astype(BF16)
    both = dot_rows(k_all[...], d_both[...])
    grads[0] = both[:, :HD]
    grads[1] = both[:, HD:]
    grads[2] = dot_rows(hid[...], gv[...])
    for j, out in enumerate((own_out,) + tuple(outs)):
        for k in range(ZQ):
            at = pl.multiple_of(row_start(s_ref, 4 + j) + row_start(s_ref, 12 + k), 16)
            for m in range(3):
                out[k, m] = grads[m, pl.ds(at, 16), :].astype(out.dtype)


def branch_of(q, u_rows, ratio):
    pre_a = dot(q, u_rows[0]) * ratio[0]
    pre_b = dot(q, u_rows[1]) * ratio[1]
    hid = (pre_a * jax.nn.sigmoid(pre_a) * pre_b).astype(BF16)
    branch = dot(hid, u_rows[2]) * ratio[2]
    squares = branch * branch
    lanes = sum(squares[:, c * 128:(c + 1) * 128] for c in range(HD // 128))
    return branch.astype(BF16), jnp.sum(lanes.T, axis=0, keepdims=True)


def apply_kernel(s_ref, q_prev, q_own, old_sq, upd, *rest):
    blocks, (f_prev, f_own, sq, new, u_rows) = rest[:XY // 2], rest[XY // 2:]
    fill_rows(s_ref, blocks, u_rows)
    ratio = [
        jnp.sqrt(old_sq[m:m + 1, :]) / jnp.sqrt(columns_sq(u_rows, m) + EPS) for m in range(3)
    ]
    for m in range(3):
        new[m] = upd[m] * ratio[m]
    f_prev[...], sq[0:1, :] = branch_of(q_prev[...], u_rows, ratio)
    f_own[...], sq[1:2, :] = branch_of(q_own[...], u_rows, ratio)


def attention_kernel(s_ref, q_ref, k_ref, v_ref, halo, *rest):
    scale = 1.0 / math.sqrt(HD)
    first = s_ref[2] == 0
    crossing = s_ref[3] == 0
    close, out = rest[:-1], rest[-1]
    half = BLK // 2
    for part in range(2):
        base = part * half
        q = q_ref[base:base + half, :]
        own_len = base + half
        prev_len = BLK - base
        k_prev, v_prev = halo[0, base:, :], halo[1, base:, :]
        if close:
            k_prev = jnp.where(crossing, close[0][0, base:, :], k_prev)
            v_prev = jnp.where(crossing, close[0][1, base:, :], v_prev)
        s_prev = dot_cols(q, k_prev) * scale
        s_own = dot_cols(q, k_ref[:own_len, :]) * scale
        row_p = lax.broadcasted_iota(jnp.int32, (half, prev_len), 0)
        col_p = lax.broadcasted_iota(jnp.int32, (half, prev_len), 1)
        keep_p = jnp.logical_and(col_p > row_p, jnp.logical_not(first))
        row_o = lax.broadcasted_iota(jnp.int32, (half, own_len), 0) + base
        col_o = lax.broadcasted_iota(jnp.int32, (half, own_len), 1)
        s_prev = jnp.where(keep_p, s_prev, NEG)
        s_own = jnp.where(col_o <= row_o, s_own, NEG)
        top = jnp.maximum(
            jnp.max(s_prev, axis=1, keepdims=True), jnp.max(s_own, axis=1, keepdims=True)
        )
        e_prev = jnp.exp(s_prev - top)
        e_own = jnp.exp(s_own - top)
        inv = 1.0 / (
            jnp.sum(e_prev, axis=1, keepdims=True) + jnp.sum(e_own, axis=1, keepdims=True)
        )
        p_prev = (e_prev * inv).astype(BF16)
        p_own = (e_own * inv).astype(BF16)
        out[base:base + half, :] = dot(p_prev, v_prev) + dot(p_own, v_ref[:own_len, :])


def mix_kernel(s_ref, f_own, f_back, attn_own, attn_other, sums, gain, out):
    inv = as_column(lax.rsqrt(sums[0:1, :] / (HEADS * HD) + EPS))
    for own_head in range(2):

        @pl.when(s_ref[0] == own_head)
        def _():
            for head in range(2):
                f, attn = (f_own, attn_own) if head == own_head else (f_back, attn_other)
                for c in range(HD // 128):
                    cols = slice(c * 128, (c + 1) * 128)
                    to = slice(head * HD + c * 128, head * HD + (c + 1) * 128)
                    branch = f[:, cols].astype(F32) * inv * gain[0:1, to]
                    out[:, to] = (attn[:, cols] + branch).astype(BF16)


def shape(dims, dtype):
    return jax.ShapeDtypeStruct(dims, dtype)


def local(queries, keys, values, rate, fast_gate, fast_up, fast_down, out_gain):
    seq_pos = lax.axis_index("seq").astype(jnp.int32)
    own = seq_pos & 1
    other = 1 - own
    zq = (seq_pos >> 1) & (ZQ - 1)
    xy = seq_pos >> 3
    scalars = jnp.stack(
        [own, other, seq_pos, seq_pos & (RING - 1)]
        + [64 * (xy ^ j) for j in range(XY)]
        + [16 * (zq ^ k) for k in range(ZQ)]
    ).astype(jnp.int32)
    even = own == 0

    def head_of(array, want_own):
        flag = even if want_own else jnp.logical_not(even)
        return jnp.where(flag, array[:, :HD], array[:, HD:])

    fast = jnp.stack([fast_gate, fast_up, fast_down])
    mine = jnp.where(even, fast[:, 0], fast[:, 1])
    theirs = jnp.where(even, fast[:, 1], fast[:, 0])
    got = move_xor(theirs, 1)
    w_pair = jnp.where(
        even, jnp.concatenate([mine, got], axis=1), jnp.concatenate([got, mine], axis=1)
    )

    rate_send = jnp.where(even, rate[1:2], rate[0:1])
    rate_mine = jnp.where(even, rate[0:1], rate[1:2])

    def gather_zq(chunk):
        return [chunk] + [move_xor(chunk, k << 1) for k in range(1, ZQ)]

    def gather_xy(block):
        pair = jnp.stack([block, move_xor(block, 1 << 3)])
        return [pair] + [move_xor(pair, j << 4) for j in range(1, XY // 2)]

    send_other = jnp.stack([head_of(keys, False), head_of(values, False)])
    send_own = jnp.stack([head_of(keys, True), head_of(values, True)])
    plane_k = to_next_plane(keys[:, HD:])
    rate_prev = ring(rate_send, 1)
    w_parts = gather_zq(after(w_pair.astype(BF16), rate_prev))
    w_block = after(jnp.stack(w_parts), plane_k)
    w_blocks = gather_xy(w_block)
    halo = ring(after(send_other, w_parts[1]), 1)
    last = (seq_pos & (RING - 1)) == RING - 1
    plane_v = to_next_plane(after(values[:, HD:], w_blocks[-1]))
    q_prev = ring(after(head_of(queries, False), halo), 1)

    def attend(pick, prev):
        return call(
            attention_kernel,
            scalars,
            [queries, keys, values] + prev,
            [head_block(pick)] * 3 + [whole((2, BLK, HD))] * len(prev),
            shape((BLK, HD), F32),
            flops=4 * BLK * 768 * HD,
        )

    block_specs = [whole((2, ZQ, 3, 16, HD))] * (XY // 2)
    grad_out = call(
        gradient_kernel,
        scalars,
        [halo, keys, values, rate_prev, rate_mine] + w_blocks,
        [whole((2, BLK, HD)), head_block(0), head_block(0), whole((1, BLK)), whole((1, BLK))]
        + block_specs,
        [shape((ZQ, 3, 16, HD), F32)] + [shape((ZQ, 3, 16, HD), BF16)] * (XY - 1) + [shape((3, HD), F32)],
        [pltpu.VMEM((3, HD, HD), BF16)]
        + [pltpu.VMEM((2 * BLK, HD), BF16)] * 3
        + [pltpu.VMEM((2 * BLK, 2 * HD), BF16)]
        + [pltpu.VMEM((3, HD, HD), F32)],
        flops=12 * 2 * BLK * HD * HD,
    )
    old_sq = grad_out[XY]
    arrived = [move_xor(grad_out[j], j << 3) for j in range(1, XY)]
    plane_own = jnp.stack([plane_k, after(plane_v, old_sq)])
    halo_other = ring(jnp.where(last, plane_own, after(send_own, q_prev)), 1)
    chunks = []
    for k in range(ZQ):
        total = grad_out[0][k] + sum(part[k].astype(F32) for part in arrived)
        chunks.append(total if k == 0 else total.astype(BF16))
    parts = [move_xor(chunks[k], k << 1) for k in range(1, ZQ)]
    parts[0] = after(parts[0], halo_other)
    upd = w_pair + chunks[0] + sum(part.astype(F32) for part in parts)
    upd_b = upd.astype(BF16)
    plane_other = to_next_plane(after(send_other, chunks[1]))
    u_block = after(jnp.stack(gather_zq(upd_b)), plane_other)
    u_blocks = gather_xy(u_block)
    closing = close_ring(after(plane_other, u_block))
    attn_other = attend(1, [halo_other])
    f_prev, f_own, sq, new = call(
        apply_kernel,
        scalars,
        [after(q_prev, attn_other), queries, old_sq, upd] + u_blocks,
        [whole((BLK, HD)), head_block(0), whole((3, HD)), whole((3, 16, HD))] + block_specs,
        [
            shape((BLK, HD), BF16),
            shape((BLK, HD), BF16),
            shape((2, BLK), F32),
            shape((3, 16, HD), F32),
        ],
        [pltpu.VMEM((3, HD, HD), BF16)],
        flops=6 * 2 * BLK * HD * HD,
    )
    f_back = ring(f_prev, -1)
    heads = lax.axis_size("head")
    totals = sq
    for k in range(1, heads):
        totals = totals + lax.ppermute(sq, "head", [(i, i ^ k) for i in range(heads)])
    attn_own = attend(0, [halo, after(closing, totals)])
    sums = totals[1:2] + after(ring(totals[0:1], -1), attn_own)
    new_mine = jnp.where(even, new[:, :8], new[:, 8:])
    new_theirs = after(move_xor(jnp.where(even, new[:, 8:], new[:, :8]), 1), f_back)
    new_all = jnp.where(
        even,
        jnp.stack([new_mine, new_theirs], axis=1),
        jnp.stack([new_theirs, new_mine], axis=1),
    )
    gain = out_gain.reshape(1, 2 * HD)
    mixed = call(
        mix_kernel,
        scalars,
        [f_own, f_back, attn_own, attn_other, sums, gain],
        [whole((BLK, HD))] * 4 + [whole((1, BLK)), whole((1, 2 * HD))],
        shape((BLK, 2 * HD), BF16),
    )
    return mixed, new_all[0], new_all[1], new_all[2]


def solution(mesh):
    tokens = P("seq", "head")
    fast = P("head", "seq", None)
    return jax.shard_map(
        local,
        mesh=mesh,
        in_specs=(tokens, tokens, tokens, P("head", "seq"), fast, fast, fast, P("head")),
        out_specs=(tokens, fast, fast, fast),
        check_vma=False,
    )
```

```python
import functools
import math

import jax
import jax.numpy as jnp
from jax import lax
from jax.experimental import pallas as pl
from jax.experimental.pallas import tpu as pltpu
from jax.sharding import PartitionSpec as P

HEADS = 8
HD = 512
BLK = 512
TILE = 512
EPS = 1e-06
NEG = -1e30
VMEM_LIMIT = 56 * 1024 * 1024
F32 = jnp.float32
BF16 = jnp.bfloat16

ZQ, XY, RING = 4, 8, 8


def move_xor(value, mask):
    n = lax.axis_size("seq")
    return lax.ppermute(value, "seq", [(i, i ^ mask) for i in range(n)])


def ring(value, step):
    n = lax.axis_size("seq")
    pairs = [(i, i - i % RING + (i + step) % RING) for i in range(n)]
    return lax.ppermute(value, "seq", pairs)


def to_next_plane(value):
    n = lax.axis_size("seq")
    return lax.ppermute(value, "seq", [(i, i + RING) for i in range(RING - 1, n - RING, RING)])


def close_ring(value):
    n = lax.axis_size("seq")
    return lax.ppermute(value, "seq", [(i, i - RING + 1) for i in range(RING - 1, n, RING)])


def after(value, other):
    return lax.optimization_barrier((value, other))[0]


def dot(a, b):
    return lax.dot_general(a, b, (((1,), (0,)), ((), ())), preferred_element_type=F32)


def dot_rows(a, b):
    return lax.dot_general(a, b, (((0,), (0,)), ((), ())), preferred_element_type=F32)


def dot_cols(a, b):
    return lax.dot_general(a, b, (((1,), (1,)), ((), ())), preferred_element_type=F32)


def whole(shape):
    rank = len(shape)
    return pl.BlockSpec(shape, lambda i, s: (0,) * rank)


def head_block(pick):
    return pl.BlockSpec((BLK, HD), lambda i, s: (0, s[pick]))


def call(kernel, scalars, ins, in_specs, outs, scratch=(), flops=0):
    multi = isinstance(outs, list)
    out_list = outs if multi else [outs]
    nbytes = sum(a.size * a.dtype.itemsize for a in ins)
    specs = [whole(o.shape) for o in out_list]
    return pl.pallas_call(
        kernel,
        out_shape=outs,
        grid_spec=pltpu.PrefetchScalarGridSpec(
            num_scalar_prefetch=1,
            grid=(1,),
            in_specs=in_specs,
            out_specs=specs if multi else specs[0],
            scratch_shapes=list(scratch),
        ),
        compiler_params=pltpu.CompilerParams(vmem_limit_bytes=VMEM_LIMIT),
        cost_estimate=pl.CostEstimate(flops=flops, transcendentals=0, bytes_accessed=nbytes),
    )(scalars, *ins)


def row_start(s_ref, index):
    return pl.multiple_of(s_ref[index], 16)


def fill_rows(s_ref, blocks, rows_ref):
    for j, block in enumerate(blocks):
        for t in range(2):
            for k in range(ZQ):
                at = row_start(s_ref, 4 + 2 * j + t) + row_start(s_ref, 12 + k)
                at = pl.multiple_of(at, 16)
                for m in range(3):
                    rows_ref[m, pl.ds(at, 16), :] = block[t, k, m]


def columns_sq(rows_ref, m):
    w = rows_ref[m].astype(F32)
    return jnp.sum(w * w, axis=0, keepdims=True)


def as_column(row):
    return jnp.broadcast_to(row, (128, row.shape[1])).T


def gradient_kernel(s_ref, halo, k_own, v_own, rate_prev, rate_own, *rest):
    blocks, rest = rest[:XY // 2], rest[XY // 2:]
    own_out, outs, old_sq = rest[0], rest[1:XY], rest[XY]
    w_rows, k_all, gv, hid, d_both, grads = rest[XY + 1:]
    fill_rows(s_ref, blocks, w_rows)
    for m in range(3):
        old_sq[m:m + 1, :] = columns_sq(w_rows, m)
    for part in range(2):
        eta_all = as_column((rate_prev if part == 0 else rate_own)[0:1, :])
        for at in range(0, BLK, TILE):
            rows = slice(part * BLK + at, part * BLK + at + TILE)
            here = slice(at, at + TILE)
            k = halo[0, here, :] if part == 0 else k_own[here, :]
            v = (halo[1, here, :] if part == 0 else v_own[here, :]).astype(F32)
            eta = eta_all[here, :]
            scaled = jnp.concatenate(
                [eta * v[:, c * 128:(c + 1) * 128] for c in range(HD // 128)], axis=1
            ).astype(BF16)
            k_all[rows, :] = k
            gv[rows, :] = scaled
            pre_a = dot(k, w_rows[0])
            pre_b = dot(k, w_rows[1])
            back = dot_cols(scaled, w_rows[2])
            sigma = jax.nn.sigmoid(pre_a)
            gated = pre_a * sigma
            hid[rows, :] = (gated * pre_b).astype(BF16)
            gate = back * pre_b * sigma * (1.0 + pre_a * (1.0 - sigma))
            d_both[rows, :HD] = gate.astype(BF16)
            d_both[rows, HD:] = (back * gated).astype(BF16)
    both = dot_rows(k_all[...], d_both[...])
    grads[0] = both[:, :HD]
    grads[1] = both[:, HD:]
    grads[2] = dot_rows(hid[...], gv[...])
    for j, out in enumerate((own_out,) + tuple(outs)):
        for k in range(ZQ):
            at = pl.multiple_of(row_start(s_ref, 4 + j) + row_start(s_ref, 12 + k), 16)
            for m in range(3):
                out[k, m] = grads[m, pl.ds(at, 16), :].astype(out.dtype)


def branch_of(q, u_rows, ratio):
    pre_a = dot(q, u_rows[0]) * ratio[0]
    pre_b = dot(q, u_rows[1]) * ratio[1]
    hid = (pre_a * jax.nn.sigmoid(pre_a) * pre_b).astype(BF16)
    branch = dot(hid, u_rows[2]) * ratio[2]
    squares = branch * branch
    lanes = sum(squares[:, c * 128:(c + 1) * 128] for c in range(HD // 128))
    return branch.astype(BF16), jnp.sum(lanes.T, axis=0, keepdims=True)


def apply_kernel(s_ref, q_prev, q_own, old_sq, upd, *rest):
    blocks, (f_prev, f_own, sq, new, u_rows) = rest[:XY // 2], rest[XY // 2:]
    fill_rows(s_ref, blocks, u_rows)
    ratio = [
        jnp.sqrt(old_sq[m:m + 1, :]) / jnp.sqrt(columns_sq(u_rows, m) + EPS) for m in range(3)
    ]
    for m in range(3):
        new[m] = upd[m] * ratio[m]
    f_prev[...], sq[0:1, :] = branch_of(q_prev[...], u_rows, ratio)
    f_own[...], sq[1:2, :] = branch_of(q_own[...], u_rows, ratio)


def attention_kernel(s_ref, q_ref, k_ref, v_ref, halo, *rest):
    scale = 1.0 / math.sqrt(HD)
    first = s_ref[2] == 0
    crossing = s_ref[3] == 0
    close, out = rest[:-1], rest[-1]
    half = BLK // 2
    for part in range(2):
        base = part * half
        q = q_ref[base:base + half, :]
        own_len = base + half
        prev_len = BLK - base
        k_prev, v_prev = halo[0, base:, :], halo[1, base:, :]
        if close:
            k_prev = jnp.where(crossing, close[0][0, base:, :], k_prev)
            v_prev = jnp.where(crossing, close[0][1, base:, :], v_prev)
        s_prev = dot_cols(q, k_prev) * scale
        s_own = dot_cols(q, k_ref[:own_len, :]) * scale
        row_p = lax.broadcasted_iota(jnp.int32, (half, prev_len), 0)
        col_p = lax.broadcasted_iota(jnp.int32, (half, prev_len), 1)
        keep_p = jnp.logical_and(col_p > row_p, jnp.logical_not(first))
        row_o = lax.broadcasted_iota(jnp.int32, (half, own_len), 0) + base
        col_o = lax.broadcasted_iota(jnp.int32, (half, own_len), 1)
        s_prev = jnp.where(keep_p, s_prev, NEG)
        s_own = jnp.where(col_o <= row_o, s_own, NEG)
        top = jnp.maximum(
            jnp.max(s_prev, axis=1, keepdims=True), jnp.max(s_own, axis=1, keepdims=True)
        )
        e_prev = jnp.exp(s_prev - top)
        e_own = jnp.exp(s_own - top)
        inv = 1.0 / (
            jnp.sum(e_prev, axis=1, keepdims=True) + jnp.sum(e_own, axis=1, keepdims=True)
        )
        p_prev = (e_prev * inv).astype(BF16)
        p_own = (e_own * inv).astype(BF16)
        out[base:base + half, :] = dot(p_prev, v_prev) + dot(p_own, v_ref[:own_len, :])


def mix_kernel(s_ref, f_own, f_back, attn_own, attn_other, sums, gain, out):
    inv = as_column(lax.rsqrt(sums[0:1, :] / (HEADS * HD) + EPS))
    for own_head in range(2):

        @pl.when(s_ref[0] == own_head)
        def _():
            for head in range(2):
                f, attn = (f_own, attn_own) if head == own_head else (f_back, attn_other)
                for c in range(HD // 128):
                    cols = slice(c * 128, (c + 1) * 128)
                    to = slice(head * HD + c * 128, head * HD + (c + 1) * 128)
                    branch = f[:, cols].astype(F32) * inv * gain[0:1, to]
                    out[:, to] = (attn[:, cols] + branch).astype(BF16)


def shape(dims, dtype):
    return jax.ShapeDtypeStruct(dims, dtype)


def local(queries, keys, values, rate, fast_gate, fast_up, fast_down, out_gain):
    seq_pos = lax.axis_index("seq").astype(jnp.int32)
    own = seq_pos & 1
    other = 1 - own
    zq = (seq_pos >> 1) & (ZQ - 1)
    xy = seq_pos >> 3
    scalars = jnp.stack(
        [own, other, seq_pos, seq_pos & (RING - 1)]
        + [64 * (xy ^ j) for j in range(XY)]
        + [16 * (zq ^ k) for k in range(ZQ)]
    ).astype(jnp.int32)
    even = own == 0

    def head_of(array, want_own):
        flag = even if want_own else jnp.logical_not(even)
        return jnp.where(flag, array[:, :HD], array[:, HD:])

    fast = jnp.stack([fast_gate, fast_up, fast_down])
    mine = jnp.where(even, fast[:, 0], fast[:, 1])
    theirs = jnp.where(even, fast[:, 1], fast[:, 0])
    got = move_xor(theirs, 1)
    w_pair = jnp.where(
        even, jnp.concatenate([mine, got], axis=1), jnp.concatenate([got, mine], axis=1)
    )

    rate_send = jnp.where(even, rate[1:2], rate[0:1])
    rate_mine = jnp.where(even, rate[0:1], rate[1:2])

    def gather_zq(chunk):
        return [chunk] + [move_xor(chunk, k << 1) for k in range(1, ZQ)]

    def gather_xy(block):
        pair = jnp.stack([block, move_xor(block, 1 << 3)])
        return [pair] + [move_xor(pair, j << 4) for j in range(1, XY // 2)]

    send_other = jnp.stack([head_of(keys, False), head_of(values, False)])
    send_own = jnp.stack([head_of(keys, True), head_of(values, True)])
    plane_k = to_next_plane(keys[:, HD:])
    rate_prev = ring(rate_send, 1)
    w_parts = gather_zq(after(w_pair.astype(BF16), rate_prev))
    w_block = after(jnp.stack(w_parts), plane_k)
    w_blocks = gather_xy(w_block)
    halo = ring(after(send_other, w_block), 1)
    last = (seq_pos & (RING - 1)) == RING - 1
    plane_v = to_next_plane(after(values[:, HD:], w_blocks[-1]))
    q_prev = ring(after(head_of(queries, False), halo), 1)

    def attend(pick, prev):
        return call(
            attention_kernel,
            scalars,
            [queries, keys, values] + prev,
            [head_block(pick)] * 3 + [whole((2, BLK, HD))] * len(prev),
            shape((BLK, HD), F32),
            flops=4 * BLK * 768 * HD,
        )

    block_specs = [whole((2, ZQ, 3, 16, HD))] * (XY // 2)
    grad_out = call(
        gradient_kernel,
        scalars,
        [halo, keys, values, rate_prev, rate_mine] + w_blocks,
        [whole((2, BLK, HD)), head_block(0), head_block(0), whole((1, BLK)), whole((1, BLK))]
        + block_specs,
        [shape((ZQ, 3, 16, HD), F32)] + [shape((ZQ, 3, 16, HD), BF16)] * (XY - 1) + [shape((3, HD), F32)],
        [pltpu.VMEM((3, HD, HD), BF16)]
        + [pltpu.VMEM((2 * BLK, HD), BF16)] * 3
        + [pltpu.VMEM((2 * BLK, 2 * HD), BF16)]
        + [pltpu.VMEM((3, HD, HD), F32)],
        flops=12 * 2 * BLK * HD * HD,
    )
    old_sq = grad_out[XY]
    arrived = [move_xor(grad_out[j], j << 3) for j in range(1, XY)]
    plane_own = jnp.stack([plane_k, after(plane_v, old_sq)])
    halo_other = ring(jnp.where(last, plane_own, after(send_own, q_prev)), 1)
    chunks = []
    for k in range(ZQ):
        total = grad_out[0][k] + sum(part[k].astype(F32) for part in arrived)
        chunks.append(total if k == 0 else total.astype(BF16))
    parts = [move_xor(after(chunks[k], halo_other), k << 1) for k in range(1, ZQ)]
    upd = w_pair + chunks[0] + sum(part.astype(F32) for part in parts)
    upd_b = upd.astype(BF16)
    plane_other = to_next_plane(after(send_other, chunks[1]))
    u_block = after(jnp.stack(gather_zq(upd_b)), plane_other)
    u_blocks = gather_xy(u_block)
    closing = close_ring(after(plane_other, u_block))
    attn_other = attend(1, [halo_other])
    f_prev, f_own, sq, new = call(
        apply_kernel,
        scalars,
        [after(q_prev, attn_other), queries, old_sq, upd] + u_blocks,
        [whole((BLK, HD)), head_block(0), whole((3, HD)), whole((3, 16, HD))] + block_specs,
        [
            shape((BLK, HD), BF16),
            shape((BLK, HD), BF16),
            shape((2, BLK), F32),
            shape((3, 16, HD), F32),
        ],
        [pltpu.VMEM((3, HD, HD), BF16)],
        flops=6 * 2 * BLK * HD * HD,
    )
    f_back = ring(f_prev, -1)
    heads = lax.axis_size("head")
    totals = sq
    for k in range(1, heads):
        totals = totals + lax.ppermute(sq, "head", [(i, i ^ k) for i in range(heads)])
    attn_own = attend(0, [halo, after(closing, totals)])
    sums = totals[1:2] + after(ring(totals[0:1], -1), attn_own)
    new_mine = jnp.where(even, new[:, :8], new[:, 8:])
    new_theirs = after(move_xor(jnp.where(even, new[:, 8:], new[:, :8]), 1), f_back)
    new_all = jnp.where(
        even,
        jnp.stack([new_mine, new_theirs], axis=1),
        jnp.stack([new_theirs, new_mine], axis=1),
    )
    gain = out_gain.reshape(1, 2 * HD)
    inv = lax.rsqrt(sums[0] / (HEADS * HD) + EPS)[:, None]
    gains = jnp.where(even, gain, jnp.roll(gain, HD, axis=1))
    mixed_own = (attn_own + f_own.astype(F32) * inv * gains[:, :HD]).astype(BF16)
    mixed_other = (attn_other + f_back.astype(F32) * inv * gains[:, HD:]).astype(BF16)
    mixed = jnp.where(
        even,
        jnp.concatenate([mixed_own, mixed_other], axis=1),
        jnp.concatenate([mixed_other, mixed_own], axis=1),
    )
    return mixed, new_all[0], new_all[1], new_all[2]


def solution(mesh):
    tokens = P("seq", "head")
    fast = P("head", "seq", None)
    return jax.shard_map(
        local,
        mesh=mesh,
        in_specs=(tokens, tokens, tokens, P("head", "seq"), fast, fast, fast, P("head")),
        out_specs=(tokens, fast, fast, fast),
        check_vma=False,
    )
```

```python
import functools
import math

import jax
import jax.numpy as jnp
from jax import lax
from jax.experimental import pallas as pl
from jax.experimental.pallas import tpu as pltpu
from jax.sharding import PartitionSpec as P

HEADS = 8
HD = 512
BLK = 512
TILE = 512
EPS = 1e-06
NEG = -1e30
VMEM_LIMIT = 40 * 1024 * 1024
F32 = jnp.float32
BF16 = jnp.bfloat16

ZQ, XY, RING = 4, 8, 8


def move_xor(value, mask):
    n = lax.axis_size("seq")
    return lax.ppermute(value, "seq", [(i, i ^ mask) for i in range(n)])


def ring(value, step):
    n = lax.axis_size("seq")
    pairs = [(i, i - i % RING + (i + step) % RING) for i in range(n)]
    return lax.ppermute(value, "seq", pairs)


def to_next_plane(value):
    n = lax.axis_size("seq")
    return lax.ppermute(value, "seq", [(i, i + RING) for i in range(RING - 1, n - RING, RING)])


def close_ring(value):
    n = lax.axis_size("seq")
    return lax.ppermute(value, "seq", [(i, i - RING + 1) for i in range(RING - 1, n, RING)])


def after(value, other):
    return lax.optimization_barrier((value, other))[0]


def dot(a, b):
    return lax.dot_general(a, b, (((1,), (0,)), ((), ())), preferred_element_type=F32)


def dot_rows(a, b):
    return lax.dot_general(a, b, (((0,), (0,)), ((), ())), preferred_element_type=F32)


def dot_cols(a, b):
    return lax.dot_general(a, b, (((1,), (1,)), ((), ())), preferred_element_type=F32)


def whole(shape):
    rank = len(shape)
    return pl.BlockSpec(shape, lambda i, s: (0,) * rank)


def head_block(pick):
    return pl.BlockSpec((BLK, HD), lambda i, s: (0, s[pick]))


IN_VMEM = pl.BlockSpec(memory_space=pltpu.VMEM)


def call(kernel, scalars, ins, in_specs, outs, scratch=(), flops=0):
    multi = isinstance(outs, list)
    out_list = outs if multi else [outs]
    nbytes = sum(a.size * a.dtype.itemsize for a in ins)
    specs = [whole(o.shape) for o in out_list]
    return pl.pallas_call(
        kernel,
        out_shape=outs,
        grid_spec=pltpu.PrefetchScalarGridSpec(
            num_scalar_prefetch=1,
            grid=(1,),
            in_specs=in_specs,
            out_specs=specs if multi else specs[0],
            scratch_shapes=list(scratch),
        ),
        compiler_params=pltpu.CompilerParams(vmem_limit_bytes=VMEM_LIMIT),
        cost_estimate=pl.CostEstimate(flops=flops, transcendentals=0, bytes_accessed=nbytes),
    )(scalars, *ins)


def row_start(s_ref, index):
    return pl.multiple_of(s_ref[index], 16)


def fill_rows(s_ref, blocks, rows_ref):
    for j, block in enumerate(blocks):
        for t in range(2):
            for k in range(ZQ):
                at = row_start(s_ref, 4 + 2 * j + t) + row_start(s_ref, 12 + k)
                at = pl.multiple_of(at, 16)
                for m in range(3):
                    rows_ref[m, pl.ds(at, 16), :] = block[t, k, m]


def columns_sq(rows_ref, m):
    w = rows_ref[m].astype(F32)
    return jnp.sum(w * w, axis=0, keepdims=True)


def as_column(row):
    return jnp.broadcast_to(row, (128, row.shape[1])).T


def gradient_kernel(s_ref, halo, k_own, v_own, rate_prev, rate_own, *rest):
    blocks, rest = rest[:XY // 2], rest[XY // 2:]
    own_out, outs, old_sq = rest[0], rest[1:XY], rest[XY]
    w_rows, k_all, gv, hid, d_both, grads = rest[XY + 1:]
    fill_rows(s_ref, blocks, w_rows)
    for m in range(3):
        old_sq[m:m + 1, :] = columns_sq(w_rows, m)
    for part in range(2):
        eta_all = as_column((rate_prev if part == 0 else rate_own)[0:1, :])
        for at in range(0, BLK, TILE):
            rows = slice(part * BLK + at, part * BLK + at + TILE)
            here = slice(at, at + TILE)
            k = halo[0, here, :] if part == 0 else k_own[here, :]
            v = (halo[1, here, :] if part == 0 else v_own[here, :]).astype(F32)
            eta = eta_all[here, :]
            scaled = jnp.concatenate(
                [eta * v[:, c * 128:(c + 1) * 128] for c in range(HD // 128)], axis=1
            ).astype(BF16)
            k_all[rows, :] = k
            gv[rows, :] = scaled
            pre_a = dot(k, w_rows[0])
            pre_b = dot(k, w_rows[1])
            back = dot_cols(scaled, w_rows[2])
            sigma = jax.nn.sigmoid(pre_a)
            gated = pre_a * sigma
            hid[rows, :] = (gated * pre_b).astype(BF16)
            gate = back * pre_b * sigma * (1.0 + pre_a * (1.0 - sigma))
            d_both[rows, :HD] = gate.astype(BF16)
            d_both[rows, HD:] = (back * gated).astype(BF16)
    both = dot_rows(k_all[...], d_both[...])
    grads[0] = both[:, :HD]
    grads[1] = both[:, HD:]
    grads[2] = dot_rows(hid[...], gv[...])
    for j, out in enumerate((own_out,) + tuple(outs)):
        for k in range(ZQ):
            at = pl.multiple_of(row_start(s_ref, 4 + j) + row_start(s_ref, 12 + k), 16)
            for m in range(3):
                out[k, m] = grads[m, pl.ds(at, 16), :].astype(out.dtype)


def branch_of(q, u_rows, ratio):
    pre_a = dot(q, u_rows[0]) * ratio[0]
    pre_b = dot(q, u_rows[1]) * ratio[1]
    hid = (pre_a * jax.nn.sigmoid(pre_a) * pre_b).astype(BF16)
    branch = dot(hid, u_rows[2]) * ratio[2]
    squares = branch * branch
    lanes = sum(squares[:, c * 128:(c + 1) * 128] for c in range(HD // 128))
    return branch.astype(BF16), jnp.sum(lanes.T, axis=0, keepdims=True)


def apply_kernel(s_ref, q_prev, q_own, old_sq, upd, *rest):
    blocks, (f_prev, f_own, sq, new, u_rows) = rest[:XY // 2], rest[XY // 2:]
    fill_rows(s_ref, blocks, u_rows)
    ratio = [
        jnp.sqrt(old_sq[m:m + 1, :]) / jnp.sqrt(columns_sq(u_rows, m) + EPS) for m in range(3)
    ]
    for m in range(3):
        new[m] = upd[m] * ratio[m]
    f_prev[...], sq[0:1, :] = branch_of(q_prev[...], u_rows, ratio)
    f_own[...], sq[1:2, :] = branch_of(q_own[...], u_rows, ratio)


def attention_kernel(s_ref, q_ref, k_ref, v_ref, halo, *rest):
    scale = 1.0 / math.sqrt(HD)
    first = s_ref[2] == 0
    crossing = s_ref[3] == 0
    close, out = rest[:-1], rest[-1]
    half = BLK // 2
    for part in range(2):
        base = part * half
        q = q_ref[base:base + half, :]
        own_len = base + half
        prev_len = BLK - base
        k_prev, v_prev = halo[0, base:, :], halo[1, base:, :]
        if close:
            k_prev = jnp.where(crossing, close[0][0, base:, :], k_prev)
            v_prev = jnp.where(crossing, close[0][1, base:, :], v_prev)
        s_prev = dot_cols(q, k_prev) * scale
        s_own = dot_cols(q, k_ref[:own_len, :]) * scale
        row_p = lax.broadcasted_iota(jnp.int32, (half, prev_len), 0)
        col_p = lax.broadcasted_iota(jnp.int32, (half, prev_len), 1)
        keep_p = jnp.logical_and(col_p > row_p, jnp.logical_not(first))
        row_o = lax.broadcasted_iota(jnp.int32, (half, own_len), 0) + base
        col_o = lax.broadcasted_iota(jnp.int32, (half, own_len), 1)
        s_prev = jnp.where(keep_p, s_prev, NEG)
        s_own = jnp.where(col_o <= row_o, s_own, NEG)
        top = jnp.maximum(
            jnp.max(s_prev, axis=1, keepdims=True), jnp.max(s_own, axis=1, keepdims=True)
        )
        e_prev = jnp.exp(s_prev - top)
        e_own = jnp.exp(s_own - top)
        inv = 1.0 / (
            jnp.sum(e_prev, axis=1, keepdims=True) + jnp.sum(e_own, axis=1, keepdims=True)
        )
        p_prev = (e_prev * inv).astype(BF16)
        p_own = (e_own * inv).astype(BF16)
        out[base:base + half, :] = dot(p_prev, v_prev) + dot(p_own, v_ref[:own_len, :])


def mix_kernel(s_ref, f_own, f_back, attn_own, attn_other, sums, gain, out):
    inv = as_column(lax.rsqrt(sums[0:1, :] / (HEADS * HD) + EPS))
    for own_head in range(2):

        @pl.when(s_ref[0] == own_head)
        def _():
            for head in range(2):
                f, attn = (f_own, attn_own) if head == own_head else (f_back, attn_other)
                for c in range(HD // 128):
                    cols = slice(c * 128, (c + 1) * 128)
                    to = slice(head * HD + c * 128, head * HD + (c + 1) * 128)
                    branch = f[:, cols].astype(F32) * inv * gain[0:1, to]
                    out[:, to] = (attn[:, cols] + branch).astype(BF16)


def shape(dims, dtype):
    return jax.ShapeDtypeStruct(dims, dtype)


def local(queries, keys, values, rate, fast_gate, fast_up, fast_down, out_gain):
    seq_pos = lax.axis_index("seq").astype(jnp.int32)
    own = seq_pos & 1
    other = 1 - own
    zq = (seq_pos >> 1) & (ZQ - 1)
    xy = seq_pos >> 3
    scalars = jnp.stack(
        [own, other, seq_pos, seq_pos & (RING - 1)]
        + [64 * (xy ^ j) for j in range(XY)]
        + [16 * (zq ^ k) for k in range(ZQ)]
    ).astype(jnp.int32)
    even = own == 0

    def head_of(array, want_own):
        flag = even if want_own else jnp.logical_not(even)
        return jnp.where(flag, array[:, :HD], array[:, HD:])

    fast = jnp.stack([fast_gate, fast_up, fast_down])
    mine = jnp.where(even, fast[:, 0], fast[:, 1])
    theirs = jnp.where(even, fast[:, 1], fast[:, 0])
    got = move_xor(theirs, 1)
    w_pair = jnp.where(
        even, jnp.concatenate([mine, got], axis=1), jnp.concatenate([got, mine], axis=1)
    )

    rate_send = jnp.where(even, rate[1:2], rate[0:1])
    rate_mine = jnp.where(even, rate[0:1], rate[1:2])

    def gather_zq(chunk):
        return [chunk] + [move_xor(chunk, k << 1) for k in range(1, ZQ)]

    def gather_xy(block):
        pair = jnp.stack([block, move_xor(block, 1 << 3)])
        return [pair] + [move_xor(pair, j << 4) for j in range(1, XY // 2)]

    send_other = jnp.stack([head_of(keys, False), head_of(values, False)])
    send_own = jnp.stack([head_of(keys, True), head_of(values, True)])
    plane_k = to_next_plane(keys[:, HD:])
    rate_prev = ring(rate_send, 1)
    w_parts = gather_zq(after(w_pair.astype(BF16), rate_prev))
    w_block = after(jnp.stack(w_parts), plane_k)
    w_blocks = gather_xy(w_block)
    halo = ring(after(send_other, w_block), 1)
    last = (seq_pos & (RING - 1)) == RING - 1
    plane_v = to_next_plane(after(values[:, HD:], w_blocks[-1]))
    q_prev = ring(after(head_of(queries, False), halo), 1)

    def attend(pick, prev):
        return call(
            attention_kernel,
            scalars,
            [queries, keys, values] + prev,
            [head_block(pick)] * 3 + [whole((2, BLK, HD))] * len(prev),
            shape((BLK, HD), F32),
            flops=4 * BLK * 768 * HD,
        )

    block_specs = [IN_VMEM] * (XY // 2)
    grad_out = call(
        gradient_kernel,
        scalars,
        [halo, keys, values, rate_prev, rate_mine] + w_blocks,
        [IN_VMEM, head_block(0), head_block(0), whole((1, BLK)), whole((1, BLK))]
        + block_specs,
        [shape((ZQ, 3, 16, HD), F32)] + [shape((ZQ, 3, 16, HD), BF16)] * (XY - 1) + [shape((3, HD), F32)],
        [pltpu.VMEM((3, HD, HD), BF16)]
        + [pltpu.VMEM((2 * BLK, HD), BF16)] * 3
        + [pltpu.VMEM((2 * BLK, 2 * HD), BF16)]
        + [pltpu.VMEM((3, HD, HD), F32)],
        flops=12 * 2 * BLK * HD * HD,
    )
    old_sq = grad_out[XY]
    arrived = [move_xor(grad_out[j], j << 3) for j in range(1, XY)]
    plane_own = jnp.stack([plane_k, after(plane_v, old_sq)])
    halo_other = ring(jnp.where(last, plane_own, after(send_own, q_prev)), 1)
    chunks = []
    for k in range(ZQ):
        total = grad_out[0][k] + sum(part[k].astype(F32) for part in arrived)
        chunks.append(total if k == 0 else total.astype(BF16))
    parts = [move_xor(after(chunks[k], halo_other), k << 1) for k in range(1, ZQ)]
    upd = w_pair + chunks[0] + sum(part.astype(F32) for part in parts)
    upd_b = upd.astype(BF16)
    plane_other = to_next_plane(after(send_other, chunks[1]))
    u_block = after(jnp.stack(gather_zq(upd_b)), plane_other)
    u_blocks = gather_xy(u_block)
    closing = close_ring(after(plane_other, u_block))
    attn_other = attend(1, [halo_other])
    f_prev, f_own, sq, new = call(
        apply_kernel,
        scalars,
        [after(q_prev, attn_other), queries, old_sq, upd] + u_blocks,
        [whole((BLK, HD)), head_block(0), whole((3, HD)), whole((3, 16, HD))] + block_specs,
        [
            shape((BLK, HD), BF16),
            shape((BLK, HD), BF16),
            shape((2, BLK), F32),
            shape((3, 16, HD), F32),
        ],
        [pltpu.VMEM((3, HD, HD), BF16)],
        flops=6 * 2 * BLK * HD * HD,
    )
    f_back = ring(f_prev, -1)
    heads = lax.axis_size("head")
    totals = sq
    for k in range(1, heads):
        totals = totals + lax.ppermute(sq, "head", [(i, i ^ k) for i in range(heads)])
    attn_own = attend(0, [halo, after(closing, totals)])
    sums = totals[1:2] + after(ring(totals[0:1], -1), attn_own)
    new_mine = jnp.where(even, new[:, :8], new[:, 8:])
    new_theirs = after(move_xor(jnp.where(even, new[:, 8:], new[:, :8]), 1), f_back)
    new_all = jnp.where(
        even,
        jnp.stack([new_mine, new_theirs], axis=1),
        jnp.stack([new_theirs, new_mine], axis=1),
    )
    gain = out_gain.reshape(1, 2 * HD)
    inv = lax.rsqrt(sums[0] / (HEADS * HD) + EPS)[:, None]
    gains = jnp.where(even, gain, jnp.roll(gain, HD, axis=1))
    mixed_own = (attn_own + f_own.astype(F32) * inv * gains[:, :HD]).astype(BF16)
    mixed_other = (attn_other + f_back.astype(F32) * inv * gains[:, HD:]).astype(BF16)
    mixed = jnp.where(
        even,
        jnp.concatenate([mixed_own, mixed_other], axis=1),
        jnp.concatenate([mixed_other, mixed_own], axis=1),
    )
    return mixed, new_all[0], new_all[1], new_all[2]


def solution(mesh):
    tokens = P("seq", "head")
    fast = P("head", "seq", None)
    return jax.shard_map(
        local,
        mesh=mesh,
        in_specs=(tokens, tokens, tokens, P("head", "seq"), fast, fast, fast, P("head")),
        out_specs=(tokens, fast, fast, fast),
        check_vma=False,
    )
```

```python
import functools
import math

import jax
import jax.numpy as jnp
from jax import lax
from jax.experimental import pallas as pl
from jax.experimental.pallas import tpu as pltpu
from jax.sharding import PartitionSpec as P

HEADS = 8
HD = 512
BLK = 512
TILE = 512
EPS = 1e-06
NEG = -1e30
VMEM_LIMIT = 40 * 1024 * 1024
F32 = jnp.float32
BF16 = jnp.bfloat16

ZQ, XY, RING = 4, 8, 8


def move_xor(value, mask):
    n = lax.axis_size("seq")
    return lax.ppermute(value, "seq", [(i, i ^ mask) for i in range(n)])


def ring(value, step):
    n = lax.axis_size("seq")
    pairs = [(i, i - i % RING + (i + step) % RING) for i in range(n)]
    return lax.ppermute(value, "seq", pairs)


def to_next_plane(value):
    n = lax.axis_size("seq")
    return lax.ppermute(value, "seq", [(i, i + RING) for i in range(RING - 1, n - RING, RING)])


def close_ring(value):
    n = lax.axis_size("seq")
    return lax.ppermute(value, "seq", [(i, i - RING + 1) for i in range(RING - 1, n, RING)])


def after(value, other):
    return lax.optimization_barrier((value, other))[0]


def dot(a, b):
    return lax.dot_general(a, b, (((1,), (0,)), ((), ())), preferred_element_type=F32)


def dot_rows(a, b):
    return lax.dot_general(a, b, (((0,), (0,)), ((), ())), preferred_element_type=F32)


def dot_cols(a, b):
    return lax.dot_general(a, b, (((1,), (1,)), ((), ())), preferred_element_type=F32)


def whole(shape):
    rank = len(shape)
    return pl.BlockSpec(shape, lambda i, s: (0,) * rank)


def head_block(pick):
    return pl.BlockSpec((BLK, HD), lambda i, s: (0, s[pick]))


IN_VMEM = pl.BlockSpec(memory_space=pltpu.VMEM)


def call(kernel, scalars, ins, in_specs, outs, scratch=(), flops=0):
    multi = isinstance(outs, list)
    out_list = outs if multi else [outs]
    nbytes = sum(a.size * a.dtype.itemsize for a in ins)
    specs = [whole(o.shape) for o in out_list]
    return pl.pallas_call(
        kernel,
        out_shape=outs,
        grid_spec=pltpu.PrefetchScalarGridSpec(
            num_scalar_prefetch=1,
            grid=(1,),
            in_specs=in_specs,
            out_specs=specs if multi else specs[0],
            scratch_shapes=list(scratch),
        ),
        compiler_params=pltpu.CompilerParams(vmem_limit_bytes=VMEM_LIMIT),
        cost_estimate=pl.CostEstimate(flops=flops, transcendentals=0, bytes_accessed=nbytes),
    )(scalars, *ins)


def row_start(s_ref, index):
    return pl.multiple_of(s_ref[index], 16)


def fill_rows(s_ref, blocks, rows_ref):
    for j, block in enumerate(blocks):
        for t in range(2):
            for k in range(ZQ):
                at = row_start(s_ref, 4 + 2 * j + t) + row_start(s_ref, 12 + k)
                at = pl.multiple_of(at, 16)
                for m in range(3):
                    rows_ref[m, pl.ds(at, 16), :] = block[t, k, m]


def columns_sq(rows_ref, m):
    w = rows_ref[m].astype(F32)
    return jnp.sum(w * w, axis=0, keepdims=True)


def as_column(row):
    return jnp.broadcast_to(row, (128, row.shape[1])).T


def gradient_kernel(s_ref, halo, k_own, v_own, rate_prev, rate_own, *rest):
    blocks, rest = rest[:XY // 2], rest[XY // 2:]
    own_out, outs, old_sq = rest[0], rest[1:XY], rest[XY]
    w_rows, k_all, gv, hid, d_both, grads = rest[XY + 1:]
    fill_rows(s_ref, blocks, w_rows)
    for m in range(3):
        old_sq[m:m + 1, :] = columns_sq(w_rows, m)
    for part in range(2):
        eta_all = as_column((rate_prev if part == 0 else rate_own)[0:1, :])
        for at in range(0, BLK, TILE):
            rows = slice(part * BLK + at, part * BLK + at + TILE)
            here = slice(at, at + TILE)
            k = halo[0, here, :] if part == 0 else k_own[here, :]
            v = (halo[1, here, :] if part == 0 else v_own[here, :]).astype(F32)
            eta = eta_all[here, :]
            scaled = jnp.concatenate(
                [eta * v[:, c * 128:(c + 1) * 128] for c in range(HD // 128)], axis=1
            ).astype(BF16)
            k_all[rows, :] = k
            gv[rows, :] = scaled
            pre_a = dot(k, w_rows[0])
            pre_b = dot(k, w_rows[1])
            back = dot_cols(scaled, w_rows[2])
            sigma = jax.nn.sigmoid(pre_a)
            gated = pre_a * sigma
            hid[rows, :] = (gated * pre_b).astype(BF16)
            gate = back * pre_b * sigma * (1.0 + pre_a * (1.0 - sigma))
            d_both[rows, :HD] = gate.astype(BF16)
            d_both[rows, HD:] = (back * gated).astype(BF16)
    both = dot_rows(k_all[...], d_both[...])
    grads[0] = both[:, :HD]
    grads[1] = both[:, HD:]
    grads[2] = dot_rows(hid[...], gv[...])
    for j, out in enumerate((own_out,) + tuple(outs)):
        for k in range(ZQ):
            at = pl.multiple_of(row_start(s_ref, 4 + j) + row_start(s_ref, 12 + k), 16)
            for m in range(3):
                out[k, m] = grads[m, pl.ds(at, 16), :].astype(out.dtype)


def branch_of(q, u_rows, ratio):
    pre_a = dot(q, u_rows[0]) * ratio[0]
    pre_b = dot(q, u_rows[1]) * ratio[1]
    hid = (pre_a * jax.nn.sigmoid(pre_a) * pre_b).astype(BF16)
    branch = dot(hid, u_rows[2]) * ratio[2]
    squares = branch * branch
    lanes = sum(squares[:, c * 128:(c + 1) * 128] for c in range(HD // 128))
    return branch.astype(BF16), jnp.sum(lanes.T, axis=0, keepdims=True)


def apply_kernel(s_ref, q_prev, q_own, old_sq, upd, *rest):
    blocks, (f_prev, f_own, sq, new, u_rows) = rest[:XY // 2], rest[XY // 2:]
    fill_rows(s_ref, blocks, u_rows)
    ratio = [
        jnp.sqrt(old_sq[m:m + 1, :]) / jnp.sqrt(columns_sq(u_rows, m) + EPS) for m in range(3)
    ]
    for m in range(3):
        new[m] = upd[m] * ratio[m]
    f_prev[...], sq[0:1, :] = branch_of(q_prev[...], u_rows, ratio)
    f_own[...], sq[1:2, :] = branch_of(q_own[...], u_rows, ratio)


def attention_kernel(s_ref, q_ref, k_ref, v_ref, halo, *rest):
    scale = 1.0 / math.sqrt(HD)
    first = s_ref[2] == 0
    crossing = s_ref[3] == 0
    close, out = rest[:-1], rest[-1]
    half = BLK // 2
    for part in range(2):
        base = part * half
        q = q_ref[base:base + half, :]
        own_len = base + half
        prev_len = BLK - base
        k_prev, v_prev = halo[0, base:, :], halo[1, base:, :]
        if close:
            k_prev = jnp.where(crossing, close[0][0, base:, :], k_prev)
            v_prev = jnp.where(crossing, close[0][1, base:, :], v_prev)
        s_prev = dot_cols(q, k_prev) * scale
        s_own = dot_cols(q, k_ref[:own_len, :]) * scale
        row_p = lax.broadcasted_iota(jnp.int32, (half, prev_len), 0)
        col_p = lax.broadcasted_iota(jnp.int32, (half, prev_len), 1)
        keep_p = jnp.logical_and(col_p > row_p, jnp.logical_not(first))
        row_o = lax.broadcasted_iota(jnp.int32, (half, own_len), 0) + base
        col_o = lax.broadcasted_iota(jnp.int32, (half, own_len), 1)
        s_prev = jnp.where(keep_p, s_prev, NEG)
        s_own = jnp.where(col_o <= row_o, s_own, NEG)
        top = jnp.maximum(
            jnp.max(s_prev, axis=1, keepdims=True), jnp.max(s_own, axis=1, keepdims=True)
        )
        e_prev = jnp.exp(s_prev - top)
        e_own = jnp.exp(s_own - top)
        inv = 1.0 / (
            jnp.sum(e_prev, axis=1, keepdims=True) + jnp.sum(e_own, axis=1, keepdims=True)
        )
        p_prev = (e_prev * inv).astype(BF16)
        p_own = (e_own * inv).astype(BF16)
        out[base:base + half, :] = dot(p_prev, v_prev) + dot(p_own, v_ref[:own_len, :])


def mix_kernel(s_ref, f_own, f_back, attn_own, attn_other, sums, gain, out):
    inv = as_column(lax.rsqrt(sums[0:1, :] / (HEADS * HD) + EPS))
    for own_head in range(2):

        @pl.when(s_ref[0] == own_head)
        def _():
            for head in range(2):
                f, attn = (f_own, attn_own) if head == own_head else (f_back, attn_other)
                for c in range(HD // 128):
                    cols = slice(c * 128, (c + 1) * 128)
                    to = slice(head * HD + c * 128, head * HD + (c + 1) * 128)
                    branch = f[:, cols].astype(F32) * inv * gain[0:1, to]
                    out[:, to] = (attn[:, cols] + branch).astype(BF16)


def shape(dims, dtype):
    return jax.ShapeDtypeStruct(dims, dtype)


def local(queries, keys, values, rate, fast_gate, fast_up, fast_down, out_gain):
    seq_pos = lax.axis_index("seq").astype(jnp.int32)
    own = seq_pos & 1
    other = 1 - own
    zq = (seq_pos >> 1) & (ZQ - 1)
    xy = seq_pos >> 3
    scalars = jnp.stack(
        [own, other, seq_pos, seq_pos & (RING - 1)]
        + [64 * (xy ^ j) for j in range(XY)]
        + [16 * (zq ^ k) for k in range(ZQ)]
    ).astype(jnp.int32)
    even = own == 0

    def head_of(array, want_own):
        flag = even if want_own else jnp.logical_not(even)
        return jnp.where(flag, array[:, :HD], array[:, HD:])

    fast = jnp.stack([fast_gate, fast_up, fast_down])
    mine = jnp.where(even, fast[:, 0], fast[:, 1])
    theirs = jnp.where(even, fast[:, 1], fast[:, 0])
    got = move_xor(theirs, 1)
    w_pair = jnp.where(
        even, jnp.concatenate([mine, got], axis=1), jnp.concatenate([got, mine], axis=1)
    )

    rate_send = jnp.where(even, rate[1:2], rate[0:1])
    rate_mine = jnp.where(even, rate[0:1], rate[1:2])

    def gather_zq(chunk):
        return [chunk] + [move_xor(chunk, k << 1) for k in range(1, ZQ)]

    def gather_xy(block):
        pair = jnp.stack([block, move_xor(block, 1 << 3)])
        return [pair] + [move_xor(pair, j << 4) for j in range(1, XY // 2)]

    send_other = jnp.stack([head_of(keys, False), head_of(values, False)])
    send_own = jnp.stack([head_of(keys, True), head_of(values, True)])
    plane_k = to_next_plane(keys[:, HD:])
    rate_prev = ring(rate_send, 1)
    w_parts = gather_zq(after(w_pair.astype(BF16), rate_prev))
    w_block = after(jnp.stack(w_parts), plane_k)
    w_blocks = gather_xy(w_block)
    halo = ring(after(send_other, w_block), 1)
    last = (seq_pos & (RING - 1)) == RING - 1
    plane_v = to_next_plane(after(values[:, HD:], w_blocks[-1]))
    q_prev = ring(after(head_of(queries, False), halo), 1)

    def attend(pick, prev):
        return call(
            attention_kernel,
            scalars,
            [queries, keys, values] + prev,
            [head_block(pick)] * 3 + [whole((2, BLK, HD))] * len(prev),
            shape((BLK, HD), F32),
            flops=4 * BLK * 768 * HD,
        )

    block_specs = [IN_VMEM] * (XY // 2)
    grad_out = call(
        gradient_kernel,
        scalars,
        [halo, keys, values, rate_prev, rate_mine] + w_blocks,
        [IN_VMEM, head_block(0), head_block(0), whole((1, BLK)), whole((1, BLK))]
        + block_specs,
        [shape((ZQ, 3, 16, HD), F32)] + [shape((ZQ, 3, 16, HD), BF16)] * (XY - 1) + [shape((3, HD), F32)],
        [pltpu.VMEM((3, HD, HD), BF16)]
        + [pltpu.VMEM((2 * BLK, HD), BF16)] * 3
        + [pltpu.VMEM((2 * BLK, 2 * HD), BF16)]
        + [pltpu.VMEM((3, HD, HD), F32)],
        flops=12 * 2 * BLK * HD * HD,
    )
    old_sq = grad_out[XY]
    arrived = [move_xor(grad_out[j], j << 3) for j in range(1, XY)]
    plane_own = jnp.stack([plane_k, after(plane_v, old_sq)])
    halo_other = ring(jnp.where(last, plane_own, after(send_own, q_prev)), 1)
    chunks = []
    for k in range(ZQ):
        total = grad_out[0][k] + sum(part[k].astype(F32) for part in arrived)
        chunks.append(total if k == 0 else total.astype(BF16))
    parts = [move_xor(after(chunks[k], halo_other), k << 1) for k in range(1, ZQ)]
    upd = w_pair + chunks[0] + sum(part.astype(F32) for part in parts)
    upd_b = upd.astype(BF16)
    plane_other = to_next_plane(after(send_other, chunks[1]))
    u_block = after(jnp.stack(gather_zq(upd_b)), plane_other)
    u_blocks = gather_xy(u_block)
    closing = close_ring(after(plane_other, u_block))
    attn_other = attend(1, [halo_other])
    f_prev, f_own, sq, new = call(
        apply_kernel,
        scalars,
        [after(q_prev, attn_other), queries, old_sq, upd] + u_blocks,
        [whole((BLK, HD)), head_block(0), whole((3, HD)), whole((3, 16, HD))] + block_specs,
        [
            shape((BLK, HD), BF16),
            shape((BLK, HD), BF16),
            shape((2, BLK), F32),
            shape((3, 16, HD), F32),
        ],
        [pltpu.VMEM((3, HD, HD), BF16)],
        flops=6 * 2 * BLK * HD * HD,
    )
    f_back = ring(f_prev, -1)
    heads = lax.axis_size("head")
    attn_own = attend(0, [halo, after(closing, sq)])
    sq = after(sq, attn_own)
    totals = sq
    for k in range(1, heads):
        totals = totals + lax.ppermute(sq, "head", [(i, i ^ k) for i in range(heads)])
    sums = totals[1:2] + ring(after(totals[0:1], f_back), -1)
    new_mine = jnp.where(even, new[:, :8], new[:, 8:])
    new_theirs = after(move_xor(jnp.where(even, new[:, 8:], new[:, :8]), 1), f_back)
    new_all = jnp.where(
        even,
        jnp.stack([new_mine, new_theirs], axis=1),
        jnp.stack([new_theirs, new_mine], axis=1),
    )
    gain = out_gain.reshape(1, 2 * HD)
    inv = lax.rsqrt(sums[0] / (HEADS * HD) + EPS)[:, None]
    gains = jnp.where(even, gain, jnp.roll(gain, HD, axis=1))
    mixed_own = (attn_own + f_own.astype(F32) * inv * gains[:, :HD]).astype(BF16)
    mixed_other = (attn_other + f_back.astype(F32) * inv * gains[:, HD:]).astype(BF16)
    mixed = jnp.where(
        even,
        jnp.concatenate([mixed_own, mixed_other], axis=1),
        jnp.concatenate([mixed_other, mixed_own], axis=1),
    )
    return mixed, new_all[0], new_all[1], new_all[2]


def solution(mesh):
    tokens = P("seq", "head")
    fast = P("head", "seq", None)
    return jax.shard_map(
        local,
        mesh=mesh,
        in_specs=(tokens, tokens, tokens, P("head", "seq"), fast, fast, fast, P("head")),
        out_specs=(tokens, fast, fast, fast),
        check_vma=False,
    )
```

```python
import functools
import math

import jax
import jax.numpy as jnp
from jax import lax
from jax.experimental import pallas as pl
from jax.experimental.pallas import tpu as pltpu
from jax.sharding import PartitionSpec as P

HEADS = 8
HD = 512
BLK = 512
TILE = 512
EPS = 1e-06
NEG = -1e30
VMEM_LIMIT = 40 * 1024 * 1024
F32 = jnp.float32
BF16 = jnp.bfloat16

ZQ, XY, RING = 4, 8, 8


def move_xor(value, mask):
    n = lax.axis_size("seq")
    return lax.ppermute(value, "seq", [(i, i ^ mask) for i in range(n)])


def ring(value, step):
    n = lax.axis_size("seq")
    pairs = [(i, i - i % RING + (i + step) % RING) for i in range(n)]
    return lax.ppermute(value, "seq", pairs)


def to_next_plane(value):
    n = lax.axis_size("seq")
    return lax.ppermute(value, "seq", [(i, i + RING) for i in range(RING - 1, n - RING, RING)])


def close_ring(value):
    n = lax.axis_size("seq")
    return lax.ppermute(value, "seq", [(i, i - RING + 1) for i in range(RING - 1, n, RING)])


def after(value, other):
    return lax.optimization_barrier((value, other))[0]


def dot(a, b):
    return lax.dot_general(a, b, (((1,), (0,)), ((), ())), preferred_element_type=F32)


def dot_rows(a, b):
    return lax.dot_general(a, b, (((0,), (0,)), ((), ())), preferred_element_type=F32)


def dot_cols(a, b):
    return lax.dot_general(a, b, (((1,), (1,)), ((), ())), preferred_element_type=F32)


def whole(shape):
    rank = len(shape)
    return pl.BlockSpec(shape, lambda i, s: (0,) * rank)


def head_block(pick):
    return pl.BlockSpec((BLK, HD), lambda i, s: (0, s[pick]))


IN_VMEM = pl.BlockSpec(memory_space=pltpu.VMEM)


def call(kernel, scalars, ins, in_specs, outs, scratch=(), flops=0):
    multi = isinstance(outs, list)
    out_list = outs if multi else [outs]
    nbytes = sum(a.size * a.dtype.itemsize for a in ins)
    specs = [whole(o.shape) for o in out_list]
    return pl.pallas_call(
        kernel,
        out_shape=outs,
        grid_spec=pltpu.PrefetchScalarGridSpec(
            num_scalar_prefetch=1,
            grid=(1,),
            in_specs=in_specs,
            out_specs=specs if multi else specs[0],
            scratch_shapes=list(scratch),
        ),
        compiler_params=pltpu.CompilerParams(vmem_limit_bytes=VMEM_LIMIT),
        cost_estimate=pl.CostEstimate(flops=flops, transcendentals=0, bytes_accessed=nbytes),
    )(scalars, *ins)


def row_start(s_ref, index):
    return pl.multiple_of(s_ref[index], 16)


def fill_rows(s_ref, blocks, rows_ref):
    for j, block in enumerate(blocks):
        for t in range(2):
            for k in range(ZQ):
                at = row_start(s_ref, 4 + 2 * j + t) + row_start(s_ref, 12 + k)
                at = pl.multiple_of(at, 16)
                for m in range(3):
                    rows_ref[m, pl.ds(at, 16), :] = block[t, k, m]


def columns_sq(rows_ref, m):
    w = rows_ref[m].astype(F32)
    return jnp.sum(w * w, axis=0, keepdims=True)


def as_column(row):
    return jnp.broadcast_to(row, (128, row.shape[1])).T


def gradient_kernel(s_ref, halo, k_own, v_own, rate_prev, rate_own, *rest):
    blocks, rest = rest[:XY // 2], rest[XY // 2:]
    own_out, outs, old_sq = rest[0], rest[1:XY], rest[XY]
    w_rows, k_all, gv, hid, d_both, grads = rest[XY + 1:]
    fill_rows(s_ref, blocks, w_rows)
    for m in range(3):
        old_sq[m:m + 1, :] = columns_sq(w_rows, m)
    for part in range(2):
        eta_all = as_column((rate_prev if part == 0 else rate_own)[0:1, :])
        for at in range(0, BLK, TILE):
            rows = slice(part * BLK + at, part * BLK + at + TILE)
            here = slice(at, at + TILE)
            k = halo[0, here, :] if part == 0 else k_own[here, :]
            v = (halo[1, here, :] if part == 0 else v_own[here, :]).astype(F32)
            eta = eta_all[here, :]
            scaled = jnp.concatenate(
                [eta * v[:, c * 128:(c + 1) * 128] for c in range(HD // 128)], axis=1
            ).astype(BF16)
            k_all[rows, :] = k
            gv[rows, :] = scaled
            pre_a = dot(k, w_rows[0])
            pre_b = dot(k, w_rows[1])
            back = dot_cols(scaled, w_rows[2])
            sigma = jax.nn.sigmoid(pre_a)
            gated = pre_a * sigma
            hid[rows, :] = (gated * pre_b).astype(BF16)
            gate = back * pre_b * sigma * (1.0 + pre_a * (1.0 - sigma))
            d_both[rows, :HD] = gate.astype(BF16)
            d_both[rows, HD:] = (back * gated).astype(BF16)
    both = dot_rows(k_all[...], d_both[...])
    grads[0] = both[:, :HD]
    grads[1] = both[:, HD:]
    grads[2] = dot_rows(hid[...], gv[...])
    for j, out in enumerate((own_out,) + tuple(outs)):
        for k in range(ZQ):
            at = pl.multiple_of(row_start(s_ref, 4 + j) + row_start(s_ref, 12 + k), 16)
            for m in range(3):
                out[k, m] = grads[m, pl.ds(at, 16), :].astype(out.dtype)


def branch_of(q, u_rows, ratio):
    pre_a = dot(q, u_rows[0]) * ratio[0]
    pre_b = dot(q, u_rows[1]) * ratio[1]
    hid = (pre_a * jax.nn.sigmoid(pre_a) * pre_b).astype(BF16)
    branch = dot(hid, u_rows[2]) * ratio[2]
    squares = branch * branch
    lanes = sum(squares[:, c * 128:(c + 1) * 128] for c in range(HD // 128))
    return branch.astype(BF16), jnp.sum(lanes.T, axis=0, keepdims=True)


def apply_kernel(s_ref, q_prev, q_own, old_sq, upd, *rest):
    blocks, (f_prev, f_own, sq, new, u_rows) = rest[:XY // 2], rest[XY // 2:]
    fill_rows(s_ref, blocks, u_rows)
    ratio = [
        jnp.sqrt(old_sq[m:m + 1, :]) / jnp.sqrt(columns_sq(u_rows, m) + EPS) for m in range(3)
    ]
    for m in range(3):
        new[m] = upd[m] * ratio[m]
    f_prev[...], sq[0:1, :] = branch_of(q_prev[...], u_rows, ratio)
    f_own[...], sq[1:2, :] = branch_of(q_own[...], u_rows, ratio)


def attention_kernel(s_ref, q_ref, k_ref, v_ref, halo, *rest):
    scale = 1.0 / math.sqrt(HD)
    first = s_ref[2] == 0
    crossing = s_ref[3] == 0
    close, out = rest[:-1], rest[-1]
    half = BLK // 2
    for part in range(2):
        base = part * half
        q = q_ref[base:base + half, :]
        own_len = base + half
        prev_len = BLK - base
        k_prev, v_prev = halo[0, base:, :], halo[1, base:, :]
        if close:
            k_prev = jnp.where(crossing, close[0][0, base:, :], k_prev)
            v_prev = jnp.where(crossing, close[0][1, base:, :], v_prev)
        s_prev = dot_cols(q, k_prev) * scale
        s_own = dot_cols(q, k_ref[:own_len, :]) * scale
        row_p = lax.broadcasted_iota(jnp.int32, (half, prev_len), 0)
        col_p = lax.broadcasted_iota(jnp.int32, (half, prev_len), 1)
        keep_p = jnp.logical_and(col_p > row_p, jnp.logical_not(first))
        row_o = lax.broadcasted_iota(jnp.int32, (half, own_len), 0) + base
        col_o = lax.broadcasted_iota(jnp.int32, (half, own_len), 1)
        s_prev = jnp.where(keep_p, s_prev, NEG)
        s_own = jnp.where(col_o <= row_o, s_own, NEG)
        top = jnp.maximum(
            jnp.max(s_prev, axis=1, keepdims=True), jnp.max(s_own, axis=1, keepdims=True)
        )
        e_prev = jnp.exp(s_prev - top)
        e_own = jnp.exp(s_own - top)
        inv = 1.0 / (
            jnp.sum(e_prev, axis=1, keepdims=True) + jnp.sum(e_own, axis=1, keepdims=True)
        )
        p_prev = (e_prev * inv).astype(BF16)
        p_own = (e_own * inv).astype(BF16)
        out[base:base + half, :] = dot(p_prev, v_prev) + dot(p_own, v_ref[:own_len, :])


def mix_kernel(s_ref, f_own, f_back, attn_own, attn_other, sums, gain, out):
    inv = as_column(lax.rsqrt(sums[0:1, :] / (HEADS * HD) + EPS))
    for own_head in range(2):

        @pl.when(s_ref[0] == own_head)
        def _():
            for head in range(2):
                f, attn = (f_own, attn_own) if head == own_head else (f_back, attn_other)
                for c in range(HD // 128):
                    cols = slice(c * 128, (c + 1) * 128)
                    to = slice(head * HD + c * 128, head * HD + (c + 1) * 128)
                    branch = f[:, cols].astype(F32) * inv * gain[0:1, to]
                    out[:, to] = (attn[:, cols] + branch).astype(BF16)


def shape(dims, dtype):
    return jax.ShapeDtypeStruct(dims, dtype)


def local(queries, keys, values, rate, fast_gate, fast_up, fast_down, out_gain):
    seq_pos = lax.axis_index("seq").astype(jnp.int32)
    own = seq_pos & 1
    other = 1 - own
    zq = (seq_pos >> 1) & (ZQ - 1)
    xy = seq_pos >> 3
    scalars = jnp.stack(
        [own, other, seq_pos, seq_pos & (RING - 1)]
        + [64 * (xy ^ j) for j in range(XY)]
        + [16 * (zq ^ k) for k in range(ZQ)]
    ).astype(jnp.int32)
    even = own == 0

    def head_of(array, want_own):
        flag = even if want_own else jnp.logical_not(even)
        return jnp.where(flag, array[:, :HD], array[:, HD:])

    fast = jnp.stack([fast_gate, fast_up, fast_down])
    mine = jnp.where(even, fast[:, 0], fast[:, 1])
    theirs = jnp.where(even, fast[:, 1], fast[:, 0])
    got = move_xor(theirs, 1)
    w_pair = jnp.where(
        even, jnp.concatenate([mine, got], axis=1), jnp.concatenate([got, mine], axis=1)
    )

    rate_send = jnp.where(even, rate[1:2], rate[0:1])
    rate_mine = jnp.where(even, rate[0:1], rate[1:2])

    def gather_zq(chunk):
        return [chunk] + [move_xor(chunk, k << 1) for k in range(1, ZQ)]

    def gather_xy(block):
        pair = jnp.stack([block, move_xor(block, 1 << 3)])
        return [pair] + [move_xor(pair, j << 4) for j in range(1, XY // 2)]

    send_other = jnp.stack([head_of(keys, False), head_of(values, False)])
    send_own = jnp.stack([head_of(keys, True), head_of(values, True)])
    plane_k = to_next_plane(keys[:, HD:])
    rate_prev = ring(rate_send, 1)
    w_parts = gather_zq(after(w_pair.astype(BF16), rate_prev))
    w_block = after(jnp.stack(w_parts), plane_k)
    w_blocks = gather_xy(w_block)
    halo = ring(after(send_other, w_block), 1)
    last = (seq_pos & (RING - 1)) == RING - 1
    plane_v = to_next_plane(after(values, w_blocks[-1])[:, HD:])
    q_prev = ring(after(head_of(queries, False), halo), 1)

    def attend(pick, prev):
        return call(
            attention_kernel,
            scalars,
            [queries, keys, values] + prev,
            [head_block(pick)] * 3 + [whole((2, BLK, HD))] * len(prev),
            shape((BLK, HD), F32),
            flops=4 * BLK * 768 * HD,
        )

    block_specs = [IN_VMEM] * (XY // 2)
    grad_out = call(
        gradient_kernel,
        scalars,
        [halo, keys, values, rate_prev, rate_mine] + w_blocks,
        [IN_VMEM, head_block(0), head_block(0), whole((1, BLK)), whole((1, BLK))]
        + block_specs,
        [shape((ZQ, 3, 16, HD), F32)] + [shape((ZQ, 3, 16, HD), BF16)] * (XY - 1) + [shape((3, HD), F32)],
        [pltpu.VMEM((3, HD, HD), BF16)]
        + [pltpu.VMEM((2 * BLK, HD), BF16)] * 3
        + [pltpu.VMEM((2 * BLK, 2 * HD), BF16)]
        + [pltpu.VMEM((3, HD, HD), F32)],
        flops=12 * 2 * BLK * HD * HD,
    )
    old_sq = grad_out[XY]
    arrived = [move_xor(grad_out[j], j << 3) for j in range(1, XY)]
    plane_own = jnp.stack([plane_k, after(plane_v, old_sq)])
    halo_other = ring(jnp.where(last, plane_own, after(send_own, q_prev)), 1)
    chunks = []
    for k in range(ZQ):
        total = grad_out[0][k] + sum(part[k].astype(F32) for part in arrived)
        chunks.append(total if k == 0 else total.astype(BF16))
    parts = [move_xor(after(chunks[k], halo_other), k << 1) for k in range(1, ZQ)]
    upd = w_pair + chunks[0] + sum(part.astype(F32) for part in parts)
    upd_b = upd.astype(BF16)
    plane_other = to_next_plane(after(send_other, chunks[1]))
    u_block = after(jnp.stack(gather_zq(upd_b)), plane_other)
    u_blocks = gather_xy(u_block)
    closing = close_ring(after(plane_other, u_block))
    attn_other = attend(1, [halo_other])
    f_prev, f_own, sq, new = call(
        apply_kernel,
        scalars,
        [after(q_prev, attn_other), queries, old_sq, upd] + u_blocks,
        [whole((BLK, HD)), head_block(0), whole((3, HD)), whole((3, 16, HD))] + block_specs,
        [
            shape((BLK, HD), BF16),
            shape((BLK, HD), BF16),
            shape((2, BLK), F32),
            shape((3, 16, HD), F32),
        ],
        [pltpu.VMEM((3, HD, HD), BF16)],
        flops=6 * 2 * BLK * HD * HD,
    )
    f_back = ring(f_prev, -1)
    heads = lax.axis_size("head")
    attn_own = attend(0, [halo, after(closing, sq)])
    sq = after(sq, attn_own)
    totals = sq
    for k in range(1, heads):
        totals = totals + lax.ppermute(sq, "head", [(i, i ^ k) for i in range(heads)])
    sums = totals[1:2] + ring(after(totals[0:1], f_back), -1)
    new_mine = jnp.where(even, new[:, :8], new[:, 8:])
    new_theirs = after(move_xor(jnp.where(even, new[:, 8:], new[:, :8]), 1), f_back)
    new_all = jnp.where(
        even,
        jnp.stack([new_mine, new_theirs], axis=1),
        jnp.stack([new_theirs, new_mine], axis=1),
    )
    gain = out_gain.reshape(1, 2 * HD)
    inv = lax.rsqrt(sums[0] / (HEADS * HD) + EPS)[:, None]
    gains = jnp.where(even, gain, jnp.roll(gain, HD, axis=1))
    mixed_own = (attn_own + f_own.astype(F32) * inv * gains[:, :HD]).astype(BF16)
    mixed_other = (attn_other + f_back.astype(F32) * inv * gains[:, HD:]).astype(BF16)
    mixed = jnp.where(
        even,
        jnp.concatenate([mixed_own, mixed_other], axis=1),
        jnp.concatenate([mixed_other, mixed_own], axis=1),
    )
    return mixed, new_all[0], new_all[1], new_all[2]


def solution(mesh):
    tokens = P("seq", "head")
    fast = P("head", "seq", None)
    return jax.shard_map(
        local,
        mesh=mesh,
        in_specs=(tokens, tokens, tokens, P("head", "seq"), fast, fast, fast, P("head")),
        out_specs=(tokens, fast, fast, fast),
        check_vma=False,
    )
```
